32 devices in a mesh: scene: 4 (over x, core), seq: 8 (over z, y).
Axes of the slice: x: 2, y: 2, z: 4, core: 2. Of those that a mesh axis runs over, the one named last changes fastest.
Arguments:
- tokens: bfloat16 [10240, 768], P(('scene', 'seq')), may hold values from -6 to 6
- scene_tokens: int32 [4], P('scene'), may hold values from 128 to 320, as said below
- cotangent: bfloat16 [10240, 768], P(('scene', 'seq')), may hold values from -6 to 6
- qkv_master: float32 [768, 2304], P(('scene', 'seq')), may hold values from -0.21875 to 0.21875
- out_master: float32 [768, 768], P(('scene', 'seq')), may hold values from -6 to 6
- up_master: float32 [768, 3072], P(('scene', 'seq')), may hold values from -0.21875 to 0.21875
- down_master: float32 [3072, 768], P(('scene', 'seq')), may hold values from -0.109375 to 0.109375
- gain_one: float32 [768], replicated, may hold values from 0.5 to 1.5
- gain_two: float32 [768], replicated, may hold values from 0.5 to 1.5
Outputs:
- mixed: bfloat16 [10240, 768], P(('scene', 'seq'))
- input_grad: float32 [10240, 768], P(('scene', 'seq'))
- qkv_grad: float32 [768, 2304], P(('scene', 'seq'))
- out_grad: float32 [768, 768], P(('scene', 'seq'))
- up_grad: float32 [768, 3072], P(('scene', 'seq'))
- down_grad: float32 [3072, 768], P(('scene', 'seq'))
- gain_one_grad: float32 [768], P(('scene', 'seq'))
- gain_two_grad: float32 [768], P(('scene', 'seq'))
The draws below stay inside these ranges and needn't reach their ends.
Inputs may be any that keep to these rules, and one draw needn't show every extreme that they name: Slots 0 to scene_tokens[s] - 1 of every device of scene s's group hold that scene's tokens, the others are padding; one scene, drawn from the seed, has all 320 slots of every device live.
All inputs are finite; a program needn't handle non-finite values.
Results may differ from the reference program's by a relative error of at most 0.02.
Values may be sent and summed in bfloat16 or wider, within the bound.
No kernel may reach another device: no remote copies, remote signals or barrier semaphores. Data moves between devices by JAX's collectives and lax.ppermute only.
A program may use at most 512 MiB of HBM per device.

```python
import jax
import jax.numpy as jnp
from jax import lax

D = 768
HEADS = 12
HEAD = 64
FF = 3072
TOK_DEV = 320
SCENES = 4
LENGTH = 2560
N_SEQ = 8


def draw_scene_tokens(key, part):
    full_group = jax.random.randint(jax.random.fold_in(key, 11), (), 0, SCENES)
    counts = jax.random.randint(jax.random.fold_in(key, 12), (SCENES,), TOK_DEV * 2 // 5, TOK_DEV // 2 + 1)
    return jnp.where(jnp.arange(SCENES) == full_group, TOK_DEV, counts).astype(jnp.int32)


def block_levels(stream_key, dims, split, smallest, high):
    level = 1.0
    for position, shards_of in split:
        heights = jax.random.uniform(jax.random.fold_in(jax.random.fold_in(stream_key, 6), position), (shards_of,), jnp.float32, smallest / len(split), high / len(split))
        level = level * jnp.repeat(jnp.exp(heights), dims[position] // shards_of).reshape((-1,) + (1,) * (len(dims) - 1 - position))
    return level


def centred(own_key, extent, scale, limit, split=(), kind=jnp.bfloat16):
    factor_of = block_levels(own_key, extent, split, -0.22, 0.18) if split else 1.0
    result = jax.random.normal(own_key, extent, jnp.float32) * scale * factor_of
    return jnp.minimum(jnp.maximum(result, -limit), limit).astype(kind)


def setup_inputs(seed: int = 0) -> dict:
    seeds = jax.random.split(jax.random.key(seed), 10)
    return {
        "tokens": centred(seeds[0], (SCENES * LENGTH, D), 1.0, 6.0, ((0, 32),)),
        "scene_tokens": draw_scene_tokens(jax.random.fold_in(seeds[9], 71), 0),
        "cotangent": centred(seeds[2], (SCENES * LENGTH, D), 1.0, 6.0, ((0, 32),)),
        "qkv_master": centred(seeds[3], (D, 3 * D), D ** -0.5, 0.21875, ((0, 32),), jnp.float32),
        "out_master": centred(seeds[4], (D, D), ((TOK_DEV * N_SEQ) ** 0.5 * (6 * D) ** -0.5), 6.0, ((0, 32),), jnp.float32),
        "up_master": centred(seeds[5], (D, FF), D ** -0.5, 0.21875, ((0, 32),), jnp.float32),
        "down_master": centred(seeds[6], (FF, D), FF ** -0.5, 0.109375, ((0, 32),), jnp.float32),
        "gain_one": jnp.clip(1.0 + 0.1 * jax.random.normal(seeds[7], (D,), jnp.float32), 0.5, 1.5),
        "gain_two": jnp.clip(1.0 + 0.1 * jax.random.normal(seeds[8], (D,), jnp.float32), 0.5, 1.5),
    }


@jax.custom_vjp
def low(v):
    return lax.optimization_barrier(v.astype(jnp.bfloat16)).astype(jnp.float32)

@jax.custom_vjp
def low_back(v):
    return v

def low_keep(v):
    return (low(v), None)

def low_pass(kept, grad):
    return (grad,)

def back_keep(v):
    return (v, None)

def back_low(kept, grad):
    return (low(grad),)
low.defvjp(low_keep, low_pass)
low_back.defvjp(back_keep, back_low)
NEG_BIG = -1e+30

def matmul(left_side, right_side):
    return jnp.dot(left_side, right_side, precision=lax.Precision.HIGHEST, preferred_element_type=jnp.float32)

def norm_rows(values, gain_vector):
    mean_value = lax.optimization_barrier(jnp.mean(values, axis=-1, keepdims=True))
    centered = values - mean_value
    variance = lax.optimization_barrier(jnp.mean(centered * centered, axis=-1, keepdims=True))
    return centered * lax.rsqrt(variance + 1e-05) * gain_vector

def scene_layer(inputs, live_keys, weights, gain_one, gain_two):
    qkv_weight, out_weight, up_weight, down_weight = weights
    length_here = inputs.shape[0]
    normed_one = low(norm_rows(inputs, gain_one))
    qkv_rows = low(low_back(matmul(normed_one, qkv_weight)))
    query_heads = qkv_rows[:, :D].reshape(length_here, HEADS, HEAD).transpose(1, 0, 2)
    key_heads = qkv_rows[:, D:2 * D].reshape(length_here, HEADS, HEAD).transpose(1, 0, 2)
    value_heads = qkv_rows[:, 2 * D:].reshape(length_here, HEADS, HEAD).transpose(1, 0, 2)

    def head_block(triple):
        query_one, key_one, value_one = triple
        scores = low_back(matmul(query_one, key_one.T) * 0.125)
        scores = jnp.where(live_keys[None, :], scores, NEG_BIG)
        highest = lax.optimization_barrier(jnp.max(scores, axis=-1, keepdims=True))
        exponent = jnp.exp(scores - highest)
        weights_now = exponent / lax.optimization_barrier(jnp.sum(exponent, axis=-1, keepdims=True))
        return matmul(low(weights_now), value_one)
    head_out = lax.map(jax.checkpoint(head_block), (query_heads, key_heads, value_heads))
    attended = low(low_back(head_out.transpose(1, 0, 2).reshape(length_here, D)))
    resid = inputs + low_back(matmul(attended, out_weight))
    normed_two = low(norm_rows(resid, gain_two))
    upper = low_back(matmul(normed_two, up_weight))
    activated = low(jax.nn.gelu(upper))
    return resid + low_back(matmul(activated, down_weight))

def reference(tokens, scene_tokens, cotangent, qkv_master, out_master, up_master, down_master, gain_one, gain_two):
    inputs = tokens.astype(jnp.float32).reshape(SCENES, LENGTH, D)
    slots = jnp.arange(LENGTH, dtype=jnp.int32) % TOK_DEV
    masks = slots[None, :] < scene_tokens[:, None]

    def forward(inputs, qkv_master, out_master, up_master, down_master, gain_one, gain_two):
        weights = (low(qkv_master), low(out_master), low(up_master), low(down_master))
        outputs = [scene_layer(inputs[scene_index], masks[scene_index], weights, gain_one, gain_two) for scene_index in range(SCENES)]
        return jnp.stack(outputs)
    mixed, pullback = jax.vjp(forward, inputs, qkv_master, out_master, up_master, down_master, gain_one, gain_two)
    start_grad = cotangent.astype(jnp.float32).reshape(SCENES, LENGTH, D) * masks[:, :, None].astype(jnp.float32)
    grads = pullback(start_grad)
    return (mixed.reshape(SCENES * LENGTH, D).astype(jnp.bfloat16), grads[0].reshape(SCENES * LENGTH, D), grads[1], grads[2], grads[3], grads[4], grads[5], grads[6])
```

```python
import functools
import math

import jax
import jax.numpy as jnp
from jax import lax
from jax.experimental import pallas as pl
from jax.experimental.pallas import tpu as pltpu
from jax.sharding import Mesh
from jax.sharding import PartitionSpec as P

HEADS = 12
HEAD = 64
LANES = 128
NEG_BIG = -1e30
EPS = 1e-05
SCALE = 0.125
EXP_SCALE = SCALE * math.log2(math.e)
VMEM_LIMIT = 60 * 1024 * 1024
F32 = jnp.float32
BF16 = jnp.bfloat16
ALL = ("a", "c", "g", "r")


def nt(left, right):
    return lax.dot_general(left, right, (((1,), (1,)), ((), ())), preferred_element_type=F32)


def nn(left, right):
    return lax.dot_general(left, right, (((1,), (0,)), ((), ())), preferred_element_type=F32)


def tn(left, right):
    return lax.dot_general(left, right, (((0,), (0,)), ((), ())), preferred_element_type=F32)


def three_parts(value):
    first = value.astype(BF16)
    rest = value - first.astype(F32)
    second = rest.astype(BF16)
    third = (rest - second.astype(F32)).astype(BF16)
    return first, second, third


def block_rows(rows):
    return 256 if rows % 256 == 0 else rows


def attention_forward_kernel(n_own, live_ref, *refs):
    n_pieces = len(refs) - 6
    pieces, weight = refs[:n_pieces], refs[n_pieces]
    out_ref, query_ref, key_ref, value_ref, out_scr = refs[n_pieces + 1 :]
    rows = pieces[0].shape[0]
    half = rows // 2
    lane = lax.broadcasted_iota(jnp.int32, (rows, HEAD), 1)
    slot = lax.broadcasted_iota(jnp.int32, (rows, HEAD), 0)
    bias = jnp.where(slot < live_ref[0], 0.0, NEG_BIG)
    key_extra = jnp.where(lane == 0, bias, jnp.where(lane < 4, 1.0, 0.0)).astype(BF16)
    value_extra = jnp.where(lane < 3, 1.0, 0.0).astype(BF16)
    query_extra = jnp.where(lane == 0, 1.0, 0.0).astype(BF16)
    for index in range(n_pieces):
        made = nn(pieces[index][...], weight[0]).astype(BF16)
        here = slice(index * rows, (index + 1) * rows)
        key_ref[0, here, :] = jnp.concatenate([made[:, HEAD : 2 * HEAD], key_extra], axis=1)
        value_ref[0, here, :] = jnp.concatenate([made[:, 2 * HEAD :], value_extra], axis=1)
        if index < n_own:
            query_ref[0, here, :] = jnp.concatenate([made[:, :HEAD], query_extra], axis=1)

    size = block_rows(rows * n_own)
    blocks = rows * n_own // size
    full = lax.broadcasted_iota(jnp.int32, (size, LANES), 1)
    keys = key_ref[0]
    values = value_ref[0]
    scores = nt(query_ref[0, :size], keys)
    for block in range(blocks):
        here = slice(block * size, (block + 1) * size)
        later = None
        if block + 1 < blocks:
            later = nt(query_ref[0, (block + 1) * size : (block + 2) * size], keys)
        highest = jnp.max(scores, axis=1, keepdims=True)
        weights = jnp.exp2((scores - highest) * EXP_SCALE).astype(BF16)
        summed = nn(weights, values)
        total = summed[:, HEAD : HEAD + 1]
        out_scr[here, :] = summed / total
        first, second, third = three_parts(-(highest + jnp.log2(total) * (1.0 / EXP_SCALE)))
        query_ref[0, here, :] = jnp.where(
            full == HEAD + 1,
            first,
            jnp.where(
                full == HEAD + 2, second, jnp.where(full == HEAD + 3, third, query_ref[0, here, :])
            ),
        )
        scores = later
    for index in range(n_own):
        base = index * rows
        upper = out_scr[base : base + half, :HEAD]
        lower = out_scr[base + half : base + rows, :HEAD]
        out_ref[index, 0] = jnp.concatenate([upper, lower], axis=1).astype(BF16)


def attention_forward(live, pieces, weight, n_own):
    heads = weight.shape[0]
    rows, width = pieces[0].shape
    n_keys = rows * len(pieces)
    n_queries = rows * n_own
    half = rows // 2
    per_head = lambda n: pl.BlockSpec((1, n, LANES), lambda h: (h, 0, 0))
    return pl.pallas_call(
        functools.partial(attention_forward_kernel, n_own),
        grid=(heads,),
        in_specs=[pl.BlockSpec(memory_space=pltpu.SMEM)]
        + [pl.BlockSpec((rows, width), lambda h: (0, 0), pipeline_mode=pl.Buffered(1)) for _ in pieces]
        + [pl.BlockSpec((1, width, 3 * HEAD), lambda h: (h, 0, 0))],
        out_specs=[
            pl.BlockSpec((n_own, 1, half, LANES), lambda h: (0, h, 0, 0)),
            per_head(n_queries),
            per_head(n_keys),
            per_head(n_keys),
        ],
        out_shape=[
            jax.ShapeDtypeStruct((n_own, heads, half, LANES), BF16),
            jax.ShapeDtypeStruct((heads, n_queries, LANES), BF16),
            jax.ShapeDtypeStruct((heads, n_keys, LANES), BF16),
            jax.ShapeDtypeStruct((heads, n_keys, LANES), BF16),
        ],
        scratch_shapes=[pltpu.VMEM((n_queries, LANES), F32)],
        compiler_params=pltpu.CompilerParams(
            dimension_semantics=("arbitrary",), vmem_limit_bytes=VMEM_LIMIT
        ),
        name="attention_forward",
    )(live, *pieces, weight)


def attention_backward_kernel(rows, n_own, out_ref, query_ref, key_ref, value_ref, *refs):
    grads = refs[:n_own]
    own_ref, send_ref, grad_query_ref, grad_scr, low_scr, key_scr, query_scr, acc_scr = refs[n_own:]
    half = rows // 2
    lane = lax.broadcasted_iota(jnp.int32, (rows, HEAD), 1)
    for index in range(n_own):
        packed = grads[index][0]
        grad = jnp.concatenate([packed[:, :HEAD], packed[:, HEAD:]], axis=0)
        packed_out = out_ref[index, 0]
        attended = jnp.concatenate([packed_out[:, :HEAD], packed_out[:, HEAD:]], axis=0)
        delta = jnp.sum(grad.astype(F32) * attended.astype(F32), axis=1, keepdims=True)
        first, second, third = three_parts(-delta)
        zeros = jnp.zeros_like(grad)
        extra = jnp.where(
            lane == 0, first, jnp.where(lane == 1, second, jnp.where(lane == 2, third, zeros))
        )
        here = slice(index * rows, (index + 1) * rows)
        grad_scr[here, :] = jnp.concatenate([grad, extra], axis=1)
        low_scr[here, :] = jnp.concatenate([zeros, grad], axis=1)
    key_scr[...] = key_ref[0].T

    size = block_rows(rows * n_own)
    blocks = rows * n_own // size
    keys = key_ref[0]
    values = value_ref[0]
    full = lax.broadcasted_iota(jnp.int32, (size, LANES), 1)

    def products(block):
        here = slice(block * size, (block + 1) * size)
        return nt(keys, query_ref[0, here, :]), nt(values, grad_scr[here, :])

    scores, change = products(0)
    for block in range(blocks):
        here = slice(block * size, (block + 1) * size)
        later = products(block + 1) if block + 1 < blocks else (None, None)
        weights = jnp.exp2(scores * EXP_SCALE)
        dscore = (weights * change).astype(BF16)
        query = query_ref[0, here, :]
        plain = jnp.where(full < HEAD, query * SCALE, jnp.zeros_like(query))
        terms = nn(
            jnp.concatenate([weights.astype(BF16), dscore], axis=1),
            jnp.concatenate([low_scr[here, :], plain], axis=0),
        )
        if block == 0:
            acc_scr[...] = terms
        else:
            acc_scr[...] += terms
        query_scr[here, :] = nn(key_scr[...], dscore).T * SCALE
        scores, change = later
    for index in range(n_own):
        base = index * rows
        upper = query_scr[base : base + half, :HEAD]
        lower = query_scr[base + half : base + rows, :HEAD]
        grad_query_ref[index, 0] = jnp.concatenate([upper, lower], axis=1).astype(BF16)
        own_ref[index, 0] = acc_scr[base : base + rows, :]
    for index in range(send_ref.shape[0]):
        base = (n_own + index) * rows
        send_ref[index, 0] = acc_scr[base : base + rows, :].astype(BF16)


def attention_backward(out, query, key, value, grads):
    n_own, heads, half, _ = out.shape
    rows = 2 * half
    n_queries, n_keys = query.shape[1], key.shape[1]
    n_send = n_keys // rows - n_own
    per_head = lambda n: pl.BlockSpec((1, n, LANES), lambda h: (h, 0, 0))
    stacked = lambda k, n: pl.BlockSpec((k, 1, n, LANES), lambda h: (0, h, 0, 0))
    return pl.pallas_call(
        functools.partial(attention_backward_kernel, rows, n_own),
        grid=(heads,),
        in_specs=[stacked(n_own, half), per_head(n_queries), per_head(n_keys), per_head(n_keys)]
        + [per_head(half) for _ in grads],
        out_specs=[stacked(n_own, rows), stacked(n_send, rows), stacked(n_own, half)],
        out_shape=[
            jax.ShapeDtypeStruct((n_own, heads, rows, LANES), F32),
            jax.ShapeDtypeStruct((n_send, heads, rows, LANES), BF16),
            jax.ShapeDtypeStruct((n_own, heads, half, LANES), BF16),
        ],
        scratch_shapes=[
            pltpu.VMEM((n_queries, LANES), BF16),
            pltpu.VMEM((n_queries, LANES), BF16),
            pltpu.VMEM((LANES, n_keys), BF16),
            pltpu.VMEM((n_queries, LANES), F32),
            pltpu.VMEM((n_keys, LANES), F32),
        ],
        compiler_params=pltpu.CompilerParams(
            dimension_semantics=("arbitrary",), vmem_limit_bytes=VMEM_LIMIT
        ),
        name="attention_backward",
    )(out, query, key, value, *grads)


def norm_rows(values, gain_vector):
    mean_value = jnp.mean(values, axis=-1, keepdims=True)
    centered = values - mean_value
    variance = jnp.mean(centered * centered, axis=-1, keepdims=True)
    inverse = lax.rsqrt(variance + EPS)
    scaled = centered * inverse
    return (scaled * gain_vector, scaled, inverse)


def norm_back(grad_result, scaled, inverse, gain_vector):
    grad_scaled = grad_result * gain_vector
    first_mean = jnp.mean(grad_scaled, axis=-1, keepdims=True)
    second_mean = jnp.mean(grad_scaled * scaled, axis=-1, keepdims=True)
    return inverse * (grad_scaled - first_mean - scaled * second_mean)


def shift(value, axis, step):
    n = lax.axis_size(axis)
    return lax.ppermute(value, axis, [(i, (i + step) % n) for i in range(n)])


def gather(value, axis):
    n = lax.axis_size(axis)
    if n == 1:
        return value[None]
    if n == 2:
        other = shift(value, axis, 1)
        first = lax.axis_index(axis) == 0
        return jnp.stack([jnp.where(first, value, other), jnp.where(first, other, value)])
    return lax.all_gather(value, axis, axis=0)


def scatter_sum(value, axis, dim):
    n = lax.axis_size(axis)
    if n == 1:
        return lax.squeeze(value, (dim,))
    if n == 2:
        me = lax.axis_index(axis)
        mine = lax.dynamic_index_in_dim(value, me, dim, keepdims=False)
        other = lax.dynamic_index_in_dim(value, 1 - me, dim, keepdims=False)
        return mine.astype(F32) + shift(other.astype(BF16), axis, 1).astype(F32)
    moved = jnp.moveaxis(value, dim, 0).astype(BF16)
    return lax.psum_scatter(moved, axis, scatter_dimension=0, tiled=False).astype(F32)


def by_owner(received, axis):
    n = lax.axis_size(axis)
    turned = jnp.stack([received[(-i) % n] for i in range(n)])
    start = (n - lax.axis_index(axis)) % n
    return lax.dynamic_slice_in_dim(jnp.concatenate([turned, turned]), start, n, axis=0)


def on_device(
    tokens,
    scene_tokens,
    cotangent,
    qkv_master,
    out_master,
    up_master,
    down_master,
    gain_one,
    gain_two,
):
    rows, width = tokens.shape
    half = rows // 2
    hidden = up_master.shape[1]
    n_a, n_c, n_g, n_r = (lax.axis_size(axis) for axis in ALL)
    n_all = n_a * n_c * n_g * n_r
    share = qkv_master.shape[0]
    wide = hidden // width
    heads = HEADS // n_g
    live_count = scene_tokens[0]
    here = lax.axis_index("g")

    inputs = tokens.astype(F32)
    normed_one, scaled_one, inverse_one = norm_rows(inputs, gain_one)
    normed_low = normed_one.astype(BF16)
    pieces = [normed_low] + [shift(normed_low, "g", -k) for k in range(1, n_g)]
    own_pieces = list(pieces)
    for j in range(1, n_r):
        pieces += [shift(piece, "r", -j) for piece in own_pieces]

    qkv_low = qkv_master.astype(BF16)
    parts = qkv_low.reshape(share, 3, n_g, heads, HEAD).transpose(2, 0, 3, 1, 4)
    parts = parts.reshape(n_g, share, heads * 3 * HEAD)
    parts = lax.all_to_all(parts, "g", 0, 0)
    parts = gather(gather(gather(parts, "r"), "c"), "a")
    parts = parts.reshape(n_a, n_c, n_r, n_g, share, heads, 3 * HEAD)
    group_weight = parts.transpose(5, 0, 1, 3, 2, 4, 6).reshape(heads, width, 3 * HEAD)

    out_low = out_master.astype(BF16)
    up_low = up_master.astype(BF16)
    packed = jnp.concatenate(
        [
            out_low,
            up_low.reshape(share, wide, width).transpose(1, 0, 2).reshape(wide * share, width),
            down_master.astype(BF16),
        ]
    )
    per_device = packed.shape[0]
    gathered = lax.all_gather(packed, ALL, axis=0)
    out_weight = gathered[:, :share].reshape(width, width)
    up_weight = (
        gathered[:, share : share * (1 + wide)]
        .reshape(n_all, wide, share, width)
        .transpose(0, 2, 1, 3)
        .reshape(width, hidden)
    )
    down_weight = gathered[:, share * (1 + wide) :].reshape(hidden, width)

    out, query, key, value = attention_forward(scene_tokens, pieces, group_weight, n_g)
    back = [out[0]] + [shift(out[k], "g", k) for k in range(1, n_g)]
    attended = (
        by_owner(back, "g")
        .reshape(n_g, heads, half, 2, HEAD)
        .transpose(3, 2, 0, 1, 4)
        .reshape(rows, width)
    )

    resid = inputs + nn(attended, out_weight)
    normed_two, scaled_two, inverse_two = norm_rows(resid, gain_two)
    normed_two_low = normed_two.astype(BF16)
    upper = nn(normed_two_low, up_weight)
    activated, gelu_back = jax.vjp(jax.nn.gelu, upper)
    activated_low = activated.astype(BF16)
    mixed = (resid + nn(activated_low, down_weight)).astype(BF16)
    local_live = jnp.arange(rows, dtype=jnp.int32) < live_count
    grad_low = jnp.where(local_live[:, None], cotangent, jnp.zeros_like(cotangent))
    grad_result = grad_low.astype(F32)
    down_grad = tn(activated_low, grad_low).astype(BF16)
    grad_upper = gelu_back(nt(grad_low, down_weight))[0].astype(BF16)
    up_grad = tn(normed_two_low, grad_upper).astype(BF16)
    grad_normed_two = nt(grad_upper, up_weight)
    grad_resid = grad_result + norm_back(grad_normed_two, scaled_two, inverse_two, gain_two)
    grad_branch = grad_resid.astype(BF16)
    out_grad = tn(attended, grad_branch).astype(BF16)
    grad_attended = nt(grad_branch, out_weight).astype(BF16)
    packed_grad = jnp.concatenate(
        [
            out_grad.reshape(n_all, share, width),
            up_grad.reshape(n_all, share, wide, width)
            .transpose(0, 2, 1, 3)
            .reshape(n_all, wide * share, width),
            down_grad.reshape(n_all, -1, width),
        ],
        axis=1,
    )
    packed_share = lax.psum_scatter(packed_grad, ALL, scatter_dimension=0, tiled=False).astype(F32)
    out_share = packed_share[:share]
    up_share = (
        packed_share[share : share * (1 + wide)]
        .reshape(wide, share, width)
        .transpose(1, 0, 2)
        .reshape(share, hidden)
    )
    down_share = packed_share[share * (1 + wide) :]

    blocks = (
        grad_attended.reshape(2, half, n_g, heads, HEAD)
        .transpose(2, 3, 1, 0, 4)
        .reshape(n_g, heads, half, LANES)
    )
    sends = by_owner(list(blocks), "g")
    grads = [sends[0]] + [shift(sends[k], "g", -k) for k in range(1, n_g)]
    own, other, grad_query = attention_backward(out, query, key, value, grads)
    for j in range(1, n_r):
        own = own + shift(other[(j - 1) * n_g : j * n_g], "r", j).astype(F32)
    grad_pieces = jnp.concatenate([own.astype(BF16), grad_query], axis=2)

    group_rows = jnp.concatenate(
        [
            grad_query.reshape(n_g, heads, half, 2, 1, HEAD).transpose(0, 3, 2, 1, 4, 5),
            own.astype(BF16).reshape(n_g, heads, 2, half, 2, HEAD).transpose(0, 2, 3, 1, 4, 5),
        ],
        axis=4,
    ).reshape(n_g * rows, heads * 3 * HEAD)
    qkv_grad = tn(jnp.concatenate(own_pieces[:1] + own_pieces[1:], axis=0), group_rows)
    qkv_grad = qkv_grad.reshape(n_a, n_c, n_g, n_r, share, heads * 3 * HEAD)
    qkv_grad = scatter_sum(scatter_sum(scatter_sum(qkv_grad, "c", 1), "a", 0), "r", 1)
    qkv_grad = lax.all_to_all(qkv_grad.astype(BF16), "g", 0, 0).astype(F32)
    qkv_share = (
        qkv_grad.reshape(n_g, share, heads, 3, HEAD)
        .transpose(1, 3, 0, 2, 4)
        .reshape(share, 3 * width)
    )

    late_low, _ = lax.optimization_barrier((qkv_low, out))
    qkv_weight = lax.all_gather(late_low, ALL, axis=0, tiled=True)
    whole = [grad_pieces[0]] + [shift(grad_pieces[k], "g", k) for k in range(1, n_g)]
    whole = by_owner(whole, "g")
    grad_qkv = jnp.concatenate(
        [
            whole[:, :, rows:]
            .reshape(n_g, heads, half, 2, HEAD)
            .transpose(3, 2, 0, 1, 4)
            .reshape(rows, width),
            whole[:, :, :rows, :HEAD].transpose(2, 0, 1, 3).reshape(rows, width),
            whole[:, :, :rows, HEAD:].transpose(2, 0, 1, 3).reshape(rows, width),
        ],
        axis=1,
    )
    grad_normed_one = nt(grad_qkv, qkv_weight)
    input_grad = grad_resid + norm_back(grad_normed_one, scaled_one, inverse_one, gain_one)

    place = lax.axis_index(ALL) * share
    own_gain_one = lax.dynamic_slice_in_dim(gain_one, place, share)
    own_gain_two = lax.dynamic_slice_in_dim(gain_two, place, share)
    first_share = jnp.sum(qkv_low.astype(F32) * qkv_share, axis=1) / own_gain_one
    second_share = jnp.sum(up_low.astype(F32) * up_share, axis=1) / own_gain_two
    return (
        mixed,
        input_grad,
        qkv_share,
        out_share,
        up_share,
        down_share,
        first_share,
        second_share,
    )


def solution(mesh):
    n_scene, n_seq = mesh.devices.shape
    n_g = math.gcd(HEADS, n_seq)
    n_c = 2 if n_scene % 2 == 0 else 1
    inner = Mesh(mesh.devices.reshape(n_scene // n_c, n_c, n_g, n_seq // n_g), ALL)
    split = P(ALL, None)
    in_specs = (split, P(("a", "c")), split, split, split, split, split, P(), P())
    out_specs = (split, split, split, split, split, split, P(ALL), P(ALL))
    return jax.shard_map(
        on_device, mesh=inner, in_specs=in_specs, out_specs=out_specs, check_vma=False
    )
```

```python
import functools
import math

import jax
import jax.numpy as jnp
from jax import lax
from jax.experimental import pallas as pl
from jax.experimental.pallas import tpu as pltpu
from jax.sharding import Mesh
from jax.sharding import PartitionSpec as P

HEADS = 12
HEAD = 64
LANES = 128
NEG_BIG = -1e30
EPS = 1e-05
SCALE = 0.125
EXP_SCALE = SCALE * math.log2(math.e)
VMEM_LIMIT = 60 * 1024 * 1024
GELU_A = math.sqrt(2.0 / math.pi)
GELU_B = 0.044715
F32 = jnp.float32
BF16 = jnp.bfloat16
ALL = ("a", "c", "g", "r")


def nt(left, right):
    return lax.dot_general(left, right, (((1,), (1,)), ((), ())), preferred_element_type=F32)


def nn(left, right):
    return lax.dot_general(left, right, (((1,), (0,)), ((), ())), preferred_element_type=F32)


def tn(left, right):
    return lax.dot_general(left, right, (((0,), (0,)), ((), ())), preferred_element_type=F32)


def three_parts(value):
    first = value.astype(BF16)
    rest = value - first.astype(F32)
    second = rest.astype(BF16)
    third = (rest - second.astype(F32)).astype(BF16)
    return first, second, third


def block_rows(rows):
    return 256 if rows % 256 == 0 else rows


def attention_forward_kernel(n_own, live_ref, *refs):
    n_pieces = len(refs) - 6
    pieces, weight = refs[:n_pieces], refs[n_pieces]
    out_ref, query_ref, key_ref, value_ref, out_scr = refs[n_pieces + 1 :]
    rows = pieces[0].shape[0]
    half = rows // 2
    lane = lax.broadcasted_iota(jnp.int32, (rows, HEAD), 1)
    slot = lax.broadcasted_iota(jnp.int32, (rows, HEAD), 0)
    bias = jnp.where(slot < live_ref[0], 0.0, NEG_BIG)
    key_extra = jnp.where(lane == 0, bias, jnp.where(lane < 4, 1.0, 0.0)).astype(BF16)
    value_extra = jnp.where(lane < 3, 1.0, 0.0).astype(BF16)
    query_extra = jnp.where(lane == 0, 1.0, 0.0).astype(BF16)
    for index in range(n_pieces):
        made = nn(pieces[index][...], weight[0]).astype(BF16)
        here = slice(index * rows, (index + 1) * rows)
        key_ref[0, here, :] = jnp.concatenate([made[:, HEAD : 2 * HEAD], key_extra], axis=1)
        value_ref[0, here, :] = jnp.concatenate([made[:, 2 * HEAD :], value_extra], axis=1)
        if index < n_own:
            query_ref[0, here, :] = jnp.concatenate([made[:, :HEAD], query_extra], axis=1)

    size = block_rows(rows * n_own)
    blocks = rows * n_own // size
    full = lax.broadcasted_iota(jnp.int32, (size, LANES), 1)
    keys = key_ref[0]
    values = value_ref[0]
    scores = nt(query_ref[0, :size], keys)
    for block in range(blocks):
        here = slice(block * size, (block + 1) * size)
        later = None
        if block + 1 < blocks:
            later = nt(query_ref[0, (block + 1) * size : (block + 2) * size], keys)
        highest = jnp.max(scores, axis=1, keepdims=True)
        weights = jnp.exp2((scores - highest) * EXP_SCALE).astype(BF16)
        summed = nn(weights, values)
        total = summed[:, HEAD : HEAD + 1]
        out_scr[here, :] = summed / total
        first, second, third = three_parts(-(highest + jnp.log2(total) * (1.0 / EXP_SCALE)))
        query_ref[0, here, :] = jnp.where(
            full == HEAD + 1,
            first,
            jnp.where(
                full == HEAD + 2, second, jnp.where(full == HEAD + 3, third, query_ref[0, here, :])
            ),
        )
        scores = later
    for index in range(n_own):
        base = index * rows
        upper = out_scr[base : base + half, :HEAD]
        lower = out_scr[base + half : base + rows, :HEAD]
        out_ref[index, 0] = jnp.concatenate([upper, lower], axis=1).astype(BF16)


def attention_forward(live, pieces, weight, n_own):
    heads = weight.shape[0]
    rows, width = pieces[0].shape
    n_keys = rows * len(pieces)
    n_queries = rows * n_own
    half = rows // 2
    per_head = lambda n: pl.BlockSpec((1, n, LANES), lambda h: (h, 0, 0))
    return pl.pallas_call(
        functools.partial(attention_forward_kernel, n_own),
        grid=(heads,),
        in_specs=[pl.BlockSpec(memory_space=pltpu.SMEM)]
        + [pl.BlockSpec((rows, width), lambda h: (0, 0), pipeline_mode=pl.Buffered(1)) for _ in pieces]
        + [pl.BlockSpec((1, width, 3 * HEAD), lambda h: (h, 0, 0))],
        out_specs=[
            pl.BlockSpec((n_own, 1, half, LANES), lambda h: (0, h, 0, 0)),
            per_head(n_queries),
            per_head(n_keys),
            per_head(n_keys),
        ],
        out_shape=[
            jax.ShapeDtypeStruct((n_own, heads, half, LANES), BF16),
            jax.ShapeDtypeStruct((heads, n_queries, LANES), BF16),
            jax.ShapeDtypeStruct((heads, n_keys, LANES), BF16),
            jax.ShapeDtypeStruct((heads, n_keys, LANES), BF16),
        ],
        scratch_shapes=[pltpu.VMEM((n_queries, LANES), F32)],
        compiler_params=pltpu.CompilerParams(
            dimension_semantics=("arbitrary",), vmem_limit_bytes=VMEM_LIMIT
        ),
        name="attention_forward",
    )(live, *pieces, weight)


def attention_backward_kernel(rows, n_own, out_ref, query_ref, key_ref, value_ref, *refs):
    grads = refs[:n_own]
    own_ref, send_ref, grad_query_ref, grad_scr, low_scr, key_scr, query_scr, acc_scr = refs[n_own:]
    half = rows // 2
    lane = lax.broadcasted_iota(jnp.int32, (rows, HEAD), 1)
    for index in range(n_own):
        packed = grads[index][0]
        grad = jnp.concatenate([packed[:, :HEAD], packed[:, HEAD:]], axis=0)
        packed_out = out_ref[index, 0]
        attended = jnp.concatenate([packed_out[:, :HEAD], packed_out[:, HEAD:]], axis=0)
        delta = jnp.sum(grad.astype(F32) * attended.astype(F32), axis=1, keepdims=True)
        first, second, third = three_parts(-delta)
        zeros = jnp.zeros_like(grad)
        extra = jnp.where(
            lane == 0, first, jnp.where(lane == 1, second, jnp.where(lane == 2, third, zeros))
        )
        here = slice(index * rows, (index + 1) * rows)
        grad_scr[here, :] = jnp.concatenate([grad, extra], axis=1)
        low_scr[here, :] = jnp.concatenate([zeros, grad], axis=1)
    key_scr[...] = key_ref[0].T

    size = block_rows(rows * n_own)
    blocks = rows * n_own // size
    keys = key_ref[0]
    values = value_ref[0]
    full = lax.broadcasted_iota(jnp.int32, (size, LANES), 1)

    def products(block):
        here = slice(block * size, (block + 1) * size)
        return nt(keys, query_ref[0, here, :]), nt(values, grad_scr[here, :])

    scores, change = products(0)
    for block in range(blocks):
        here = slice(block * size, (block + 1) * size)
        later = products(block + 1) if block + 1 < blocks else (None, None)
        weights = jnp.exp2(scores * EXP_SCALE)
        dscore = (weights * change).astype(BF16)
        query = query_ref[0, here, :]
        plain = jnp.where(full < HEAD, query * SCALE, jnp.zeros_like(query))
        terms = nn(
            jnp.concatenate([weights.astype(BF16), dscore], axis=1),
            jnp.concatenate([low_scr[here, :], plain], axis=0),
        )
        if block == 0:
            acc_scr[...] = terms
        else:
            acc_scr[...] += terms
        query_scr[here, :] = nn(key_scr[...], dscore).T * SCALE
        scores, change = later
    for index in range(n_own):
        base = index * rows
        upper = query_scr[base : base + half, :HEAD]
        lower = query_scr[base + half : base + rows, :HEAD]
        grad_query_ref[index] = jnp.concatenate([upper, lower], axis=1).astype(BF16)
        own_ref[index] = acc_scr[base : base + rows, :]
    for index in range(send_ref.shape[0]):
        base = (n_own + index) * rows
        send_ref[index] = acc_scr[base : base + rows, :].astype(BF16)


def attention_backward(out, query, key, value, grads, head):
    n_own, _, half, _ = out.shape
    rows = 2 * half
    n_queries, n_keys = query.shape[1], key.shape[1]
    n_send = n_keys // rows - n_own
    per_head = lambda n: pl.BlockSpec((1, n, LANES), lambda i: (head, 0, 0))
    stacked = lambda k, n: pl.BlockSpec((k, 1, n, LANES), lambda i: (0, head, 0, 0))
    vmem = pl.BlockSpec(memory_space=pltpu.VMEM)
    return pl.pallas_call(
        functools.partial(attention_backward_kernel, rows, n_own),
        grid=(1,),
        in_specs=[stacked(n_own, half), per_head(n_queries), per_head(n_keys), per_head(n_keys)]
        + [per_head(half) for _ in grads],
        out_specs=[vmem, vmem, vmem],
        out_shape=[
            jax.ShapeDtypeStruct((n_own, rows, LANES), F32),
            jax.ShapeDtypeStruct((n_send, rows, LANES), BF16),
            jax.ShapeDtypeStruct((n_own, half, LANES), BF16),
        ],
        scratch_shapes=[
            pltpu.VMEM((n_queries, LANES), BF16),
            pltpu.VMEM((n_queries, LANES), BF16),
            pltpu.VMEM((LANES, n_keys), BF16),
            pltpu.VMEM((n_queries, LANES), F32),
            pltpu.VMEM((n_keys, LANES), F32),
        ],
        compiler_params=pltpu.CompilerParams(
            dimension_semantics=("arbitrary",), vmem_limit_bytes=VMEM_LIMIT
        ),
        name="attention_backward",
    )(out, query, key, value, *grads)


def unpack_rows(packed):
    heads = packed.shape[0]
    return jnp.concatenate(
        [
            jnp.concatenate([packed[h, :, :HEAD], packed[h, :, HEAD:]], axis=0)
            for h in range(heads)
        ],
        axis=1,
    )


def middle_kernel(sizes, scalar_ref, *refs):
    n_g, wide, width, rows, n_a, chunks = sizes
    refs = list(refs)

    def take(count):
        taken = refs[:count]
        del refs[:count]
        return taken

    token_ref, cotangent_ref, gain_ref = take(3)
    pieces = take(n_g)
    (weight_hbm,) = take(1)
    mixed_ref, resid_ref = take(2)
    grads = take(n_g)
    grad_hbm = [take(2 * n_a) for _ in chunks]
    weight_scr, made_scr, attended_scr, in_sem, out_sem = refs
    half = rows // 2
    part = width // n_g
    heads = part // HEAD
    block = width // (2 * n_a)
    here_a, here_c = scalar_ref[3], scalar_ref[2]

    def row_block(step_a, step_c):
        at_a = here_a + step_a
        at_a = jnp.where(at_a >= n_a, at_a - n_a, at_a)
        at_c = jnp.where(here_c + step_c >= 2, 0, here_c + step_c)
        return pl.ds(pl.multiple_of((at_a * 2 + at_c) * block, block), block)

    def chunk_of(index):
        first = 0
        for number, count in enumerate(chunks):
            if index < first + count:
                return number, pl.ds((index - first) * width, width)
            first += count

    def fetch(index):
        return [
            pltpu.make_async_copy(
                weight_hbm.at[:, pl.ds(index * width, width)],
                weight_scr.at[index],
                in_sem.at[index],
            )
        ]

    def flush(index):
        number, columns = chunk_of(index)
        return [
            pltpu.make_async_copy(
                made_scr.at[index, row_block(step_a, step_c)],
                grad_hbm[number][step_c * n_a + step_a].at[:, columns],
                out_sem.at[index, step_c * n_a + step_a],
            )
            for step_c in range(2)
            for step_a in range(n_a)
        ]

    def start(copies):
        for copy in copies:
            copy.start()

    def wait(copies):
        for copy in copies:
            copy.wait()

    count = 1 + 2 * wide
    for index in range(count):
        start(fetch(index))

    def places(k):
        at = scalar_ref[1] - k
        at = jnp.where(at < 0, at + n_g, at)
        return pl.ds(pl.multiple_of(at * part, part), part)

    resid = token_ref[...].astype(F32)
    for k in range(n_g):
        attended_scr[k] = unpack_rows(pieces[k][...])
    wait(fetch(0))
    for k in range(n_g):
        resid = resid + nn(attended_scr[k], weight_scr[0, places(k), :])
    gain = gain_ref[...]
    mean = jnp.mean(resid, axis=1, keepdims=True)
    centered = resid - mean
    inverse = lax.rsqrt(jnp.mean(centered * centered, axis=1, keepdims=True) + EPS)
    scaled = centered * inverse
    normed = (scaled * gain).astype(BF16)
    slot = lax.broadcasted_iota(jnp.int32, (rows, width), 0)
    grad_low = jnp.where(
        slot < scalar_ref[0], cotangent_ref[...].astype(F32), 0.0
    ).astype(BF16)
    normed_turned = normed.T
    added = None
    grad_normed = None
    for q in range(wide):
        up_at, down_at = 1 + 2 * q, 2 + 2 * q
        wait(fetch(up_at))
        upper = nn(normed, weight_scr[up_at])
        wait(fetch(down_at))
        grad_active = nt(grad_low, weight_scr[down_at])
        square = upper * upper
        inner = jnp.tanh((GELU_A * upper) * (1.0 + GELU_B * square))
        onward = 0.5 * (1.0 + inner)
        active = (upper * onward).astype(BF16)
        slope = onward + (0.5 * GELU_A) * upper * (1.0 - inner * inner) * (
            1.0 + (3.0 * GELU_B) * square
        )
        grad_upper = (grad_active * slope).astype(BF16)
        more = nn(active, weight_scr[down_at])
        added = more if added is None else added + more
        made_scr[down_at] = tn(active, grad_low).astype(BF16)
        start(flush(down_at))
        made_scr[up_at] = nn(normed_turned, grad_upper).astype(BF16)
        start(flush(up_at))
        more = nt(grad_upper, weight_scr[up_at])
        grad_normed = more if grad_normed is None else grad_normed + more
    mixed_ref[...] = (resid + added).astype(BF16)
    grad_scaled = grad_normed * gain
    first = jnp.mean(grad_scaled, axis=1, keepdims=True)
    second = jnp.mean(grad_scaled * scaled, axis=1, keepdims=True)
    grad_resid = grad_low.astype(F32) + inverse * (grad_scaled - first - scaled * second)
    resid_ref[...] = grad_resid
    branch = grad_resid.astype(BF16)
    for k in range(n_g):
        grad_block = nt(branch, weight_scr[0, places(k), :])
        for h in range(heads):
            here = slice(h * HEAD, (h + 1) * HEAD)
            grads[k][h] = jnp.concatenate(
                [grad_block[:half, here], grad_block[half:, here]], axis=1
            ).astype(BF16)
    for k in range(n_g):
        made_scr[0, places(k), :] = tn(attended_scr[k], branch).astype(BF16)
    start(flush(0))
    for index in range(count):
        wait(flush(index))


def middle(scalars, tokens, cotangent, gain, pieces, weights, n_a):
    rows, width = tokens.shape
    n_g = len(pieces)
    count = weights.shape[1] // width
    wide = (count - 1) // 2
    chunks = (1 + 2 * (wide // 2), 2 * (wide - wide // 2))
    vmem = pl.BlockSpec(memory_space=pltpu.VMEM)
    anywhere = pl.BlockSpec(memory_space=pl.ANY)
    flat = [
        jax.ShapeDtypeStruct((width // (2 * n_a), chunk * width), BF16)
        for chunk in chunks
        for _ in range(2 * n_a)
    ]
    return pl.pallas_call(
        functools.partial(middle_kernel, (n_g, wide, width, rows, n_a, chunks)),
        in_specs=[pl.BlockSpec(memory_space=pltpu.SMEM)] + [vmem] * (3 + n_g) + [anywhere],
        out_specs=[vmem] * (2 + n_g) + [anywhere] * len(flat),
        out_shape=[
            jax.ShapeDtypeStruct((rows, width), BF16),
            jax.ShapeDtypeStruct((rows, width), F32),
        ]
        + [jax.ShapeDtypeStruct(piece.shape, BF16) for piece in pieces]
        + flat,
        scratch_shapes=[
            pltpu.VMEM((count, width, width), BF16),
            pltpu.VMEM((count, width, width), BF16),
            pltpu.VMEM((n_g, rows, width // n_g), BF16),
            pltpu.SemaphoreType.DMA((count,)),
            pltpu.SemaphoreType.DMA((count, 2 * n_a)),
        ],
        compiler_params=pltpu.CompilerParams(vmem_limit_bytes=VMEM_LIMIT),
        name="middle",
    )(scalars, tokens, cotangent, gain, *pieces, weights)


def combine_kernel(rows, n_terms, own_ref, query_ref, *refs):
    terms, outs = refs[:n_terms], refs[n_terms:]
    for k, out_ref in enumerate(outs):
        total = own_ref[k]
        for term in terms:
            total = total + term[k].astype(F32)
        out_ref[:rows, :] = total.astype(BF16)
        out_ref[rows:, :] = query_ref[k]


def combine(own, grad_query, terms):
    n_g, rows, _ = own.shape
    vmem = pl.BlockSpec(memory_space=pltpu.VMEM)
    shape = (rows + grad_query.shape[1], LANES)
    return pl.pallas_call(
        functools.partial(combine_kernel, rows, len(terms)),
        in_specs=[vmem] * (2 + len(terms)),
        out_specs=[vmem] * n_g,
        out_shape=[jax.ShapeDtypeStruct(shape, BF16)] * n_g,
        compiler_params=pltpu.CompilerParams(vmem_limit_bytes=VMEM_LIMIT),
        name="combine",
    )(own, grad_query, *terms)


def unpack_grads(pieces, rows):
    parts = []
    for piece in pieces:
        packed = piece[rows:, :]
        parts.append(jnp.concatenate([packed[:, :HEAD], packed[:, HEAD:]], axis=0))
        parts.append(piece[:rows, :])
    return jnp.concatenate(parts, axis=1)


def group_grad_kernel(n_g, n_a, scalar_ref, *refs):
    inputs, pieces = refs[:n_g], refs[n_g:-3]
    mine_ref, other_ref, scr = refs[-3:]
    heads = len(pieces) // n_g
    rows = inputs[0].shape[0]
    left = jnp.concatenate([ref[...] for ref in inputs], axis=0)
    right = [
        unpack_grads([ref[...] for ref in pieces[k * heads : (k + 1) * heads]], rows)
        for k in range(n_g)
    ]
    right = jnp.concatenate(right, axis=0)
    scr[...] = tn(left, right)
    block = mine_ref.shape[1]
    n_c = scr.shape[0] // (n_a * block)
    for a in range(n_a):
        mine = pl.ds(pl.multiple_of((a * n_c + scalar_ref[2]) * block, block), block)
        other = pl.ds(pl.multiple_of((a * n_c + n_c - 1 - scalar_ref[2]) * block, block), block)
        mine_ref[a] = scr[mine, :]
        other_ref[a] = scr[other, :].astype(BF16)


def group_grad(scalars, inputs, pieces, n_a, n_c):
    rows, width = inputs[0].shape
    n_g = len(pieces)
    heads = len(pieces[0])
    columns = heads * 3 * HEAD
    block = width // (n_a * n_c)
    vmem = pl.BlockSpec(memory_space=pltpu.VMEM)
    return pl.pallas_call(
        functools.partial(group_grad_kernel, n_g, n_a),
        in_specs=[pl.BlockSpec(memory_space=pltpu.SMEM)] + [vmem] * (n_g * (1 + heads)),
        out_specs=[vmem] * 2,
        out_shape=[
            jax.ShapeDtypeStruct((n_a, block, columns), F32),
            jax.ShapeDtypeStruct((n_a, block, columns), BF16),
        ],
        scratch_shapes=[pltpu.VMEM((width, columns), F32)],
        compiler_params=pltpu.CompilerParams(vmem_limit_bytes=VMEM_LIMIT),
        name="group_grad",
    )(scalars, *inputs, *(piece for some in pieces for piece in some))


def input_grad_kernel(n_g, scalar_ref, token_ref, resid_ref, gain_ref, weight_ref, *refs):
    pieces, (out_ref, scr) = refs[:-2], refs[-2:]
    heads = len(pieces) // n_g
    rows, width = token_ref.shape
    padded = scr.shape[2]
    for k in range(n_g):
        at = scalar_ref[1] - k
        at = jnp.where(at < 0, at + n_g, at)
        made = unpack_grads([ref[...] for ref in pieces[k * heads : (k + 1) * heads]], rows)
        pad = jnp.zeros((rows, padded - made.shape[1]), BF16)
        scr[at] = jnp.concatenate([made, pad], axis=1)
    grad = nt(scr[0], weight_ref[:, :padded])
    for k in range(1, n_g):
        grad = grad + nt(scr[k], weight_ref[:, k * padded : (k + 1) * padded])
    values = token_ref[...].astype(F32)
    mean = jnp.mean(values, axis=1, keepdims=True)
    centered = values - mean
    inverse = lax.rsqrt(jnp.mean(centered * centered, axis=1, keepdims=True) + EPS)
    scaled = centered * inverse
    grad_scaled = grad * gain_ref[...]
    first = jnp.mean(grad_scaled, axis=1, keepdims=True)
    second = jnp.mean(grad_scaled * scaled, axis=1, keepdims=True)
    out_ref[...] = resid_ref[...] + inverse * (grad_scaled - first - scaled * second)


def input_gradient(scalars, tokens, grad_resid, gain, weight, pieces):
    rows, width = tokens.shape
    n_g = len(pieces)
    flat = [piece for some in pieces for piece in some]
    vmem = pl.BlockSpec(memory_space=pltpu.VMEM)
    return pl.pallas_call(
        functools.partial(input_grad_kernel, n_g),
        in_specs=[pl.BlockSpec(memory_space=pltpu.SMEM)] + [vmem] * (4 + len(flat)),
        out_specs=vmem,
        out_shape=jax.ShapeDtypeStruct((rows, width), F32),
        scratch_shapes=[pltpu.VMEM((n_g, rows, weight.shape[1] // n_g), BF16)],
        compiler_params=pltpu.CompilerParams(vmem_limit_bytes=VMEM_LIMIT),
        name="input_gradient",
    )(scalars, tokens, grad_resid, gain, weight, *flat)


def norm_rows(values, gain_vector):
    mean_value = jnp.mean(values, axis=-1, keepdims=True)
    centered = values - mean_value
    variance = jnp.mean(centered * centered, axis=-1, keepdims=True)
    return centered * lax.rsqrt(variance + EPS) * gain_vector


def shift(value, axis, step):
    n = lax.axis_size(axis)
    return lax.ppermute(value, axis, [(i, (i + step) % n) for i in range(n)])


def gather(value, axis):
    n = lax.axis_size(axis)
    if n == 1:
        return value[None]
    if n == 2:
        other = shift(value, axis, 1)
        first = lax.axis_index(axis) == 0
        return jnp.stack([jnp.where(first, value, other), jnp.where(first, other, value)])
    return lax.all_gather(value, axis, axis=0)


def after(value, *others):
    return lax.optimization_barrier((value,) + others)[0]


def add_high(*terms):
    total = terms[0].astype(F32)
    for term in terms[1:]:
        total = total + term.astype(F32)
    return total


def add_low(*terms):
    return add_high(*terms).astype(BF16)


def halves(value, axis, dim):
    n = lax.axis_size(axis)
    me = lax.axis_index(axis)
    mine = lax.dynamic_index_in_dim(value, me, dim, keepdims=False)
    others = [
        lax.dynamic_index_in_dim(value, (me + j) % n, dim, keepdims=False).astype(BF16)
        for j in range(1, n)
    ]
    return mine, others


def sum_halves(mine, others, axis):
    return add_high(mine, *(shift(other, axis, j) for j, other in enumerate(others, 1)))


def scatter_sum(value, axis, dim):
    return sum_halves(*halves(value, axis, dim), axis)


def on_device(
    tokens,
    scene_tokens,
    cotangent,
    qkv_master,
    out_master,
    up_master,
    down_master,
    gain_one,
    gain_two,
):
    rows, width = tokens.shape
    hidden = up_master.shape[1]
    n_a, n_c, n_g, n_r = (lax.axis_size(axis) for axis in ALL)
    share = qkv_master.shape[0]
    wide = hidden // width
    heads = HEADS // n_g
    live_count = scene_tokens[0]

    normed_low = norm_rows(tokens.astype(F32), gain_one).astype(BF16)
    qkv_low = qkv_master.astype(BF16)
    parts = qkv_low.reshape(share, 3, n_g, heads, HEAD).transpose(2, 0, 3, 1, 4)
    parts = parts.reshape(n_g, share, heads * 3 * HEAD)
    own_pieces = [normed_low] * n_g
    for k in {1, n_g - 1}:
        own_pieces[k] = shift(normed_low, "g", -k)
    ready = [own_pieces[1], own_pieces[n_g - 1]]
    others = {(j, 0): shift(normed_low, "r", -j) for j in range(1, n_r)}
    ready += others.values()
    parts = lax.all_to_all(parts, "g", 0, 0)
    ready.append(parts)
    for k in range(2, n_g - 1):
        own_pieces[k] = shift(after(own_pieces[k - 1], *ready), "g", -1)
    for k in sorted(range(1, n_g), key=lambda k: min(k, n_g - k)):
        for j in range(1, n_r):
            others[j, k] = shift(after(own_pieces[k], *ready), "r", -j)
    pieces = own_pieces + [others[at] for at in sorted(others)]

    n_all = n_a * n_c * n_g * n_r
    up_low = up_master.astype(BF16)
    up_turned = (
        up_low.reshape(share, n_all, wide, share).transpose(0, 2, 1, 3).reshape(share, wide, width)
    )
    down_turned = down_master.astype(BF16).reshape(wide, share, width)
    blocks = [out_master.astype(BF16)]
    for q in range(wide):
        blocks += [up_turned[:, q], down_turned[q]]
    weights = lax.all_gather(jnp.concatenate(blocks, axis=1), ALL, axis=0, tiled=True)

    parts = gather(gather(gather(after(parts, *ready), "r"), "c"), "a")
    parts = parts.reshape(n_a, n_c, n_r, n_g, share, heads, 3 * HEAD)
    group_weight = parts.transpose(5, 0, 1, 3, 2, 4, 6).reshape(heads, width, 3 * HEAD)

    scalars = jnp.stack(
        [live_count, lax.axis_index("g"), lax.axis_index("c"), lax.axis_index("a")]
    )
    out, query, key, value = attention_forward(scene_tokens, pieces, group_weight, n_g)
    back = [out[0]] + [shift(out[k], "g", k) for k in range(1, n_g)]
    made = middle(scalars, tokens, cotangent, gain_two[None], back, weights, n_a)
    mixed, grad_resid, sends = made[0], made[1], made[2 : 2 + n_g]
    grad_blocks = [made[2 + n_g : 2 + n_g + n_a * n_c], made[2 + n_g + n_a * n_c :]]

    terms = [[(block, shift(there, "c", 1)) for block, there in zip(some[:n_a], some[n_a:])] for some in grad_blocks]
    far = [add_low(*pair) for pair in terms[0][1:]]
    near = jnp.stack([add_high(*pair).reshape(n_g, n_r, share, -1) for pair in terms[1]])
    mine, other = halves(near, "r", 2)

    columns = heads * 3 * HEAD
    padded = -(-columns // LANES) * LANES
    turned = qkv_low.reshape(share, 3, n_g, heads, HEAD).transpose(0, 2, 3, 1, 4)
    turned = jnp.pad(turned.reshape(share, n_g, columns), ((0, 0), (0, 0), (0, padded - columns)))
    turned = after(turned.reshape(share, n_g * padded), *ready)
    qkv_weight = lax.all_gather(turned, ALL, axis=0, tiled=True)

    grads = [sends[0]] + [shift(sends[k], "g", -k) for k in range(1, n_g)]
    gate = [*far, *other]
    far = [shift(block, "a", k) for k, block in enumerate(far, 1)]
    other = [shift(block, "r", j) for j, block in enumerate(other, 1)]

    made = []
    grad_pieces = []
    whole = []

    def finish(head):
        own, across, grad_query = made[head]
        own = after(own, made[min(head + 1, heads - 1)][0])
        if head >= 2:
            own = after(own, *whole[head - 2])
        done = combine(own, grad_query, across)
        grad_pieces.append(done)
        whole.append([done[0]] + [shift(done[k], "g", k) for k in range(1, n_g)])

    for head in range(heads):
        if head == 1:
            gate = [made[0][0]]
        if head >= 2:
            finish(head - 2)
            gate = [*grad_pieces[head - 2], qkv_weight]
        if head == 2:
            first = add_high(*terms[0][0], *(after(block, made[1][0], *made[0][1]) for block in far))
            first, send = halves(first.reshape(n_g, n_r, share, -1), "r", 1)
            gate += send
            send = [shift(block, "r", j) for j, block in enumerate(send, 1)]
        gated = [after(grads[0], *gate)] + grads[1:]
        own, across, grad_query = attention_backward(out, query, key, value, gated, head)
        across = [
            shift(across[(j - 1) * n_g : j * n_g] if n_r > 2 else across, "r", j)
            for j in range(1, n_r)
        ]
        made.append((own, across, grad_query))
    finish(heads - 2)
    first = add_high(first, *(after(block, *made[-1][1]) for block in send)).astype(BF16)
    near = add_high(mine, *(after(block, *made[-1][1]) for block in other))
    second = add_low(near[0], *(shift(near[k].astype(BF16), "a", k) for k in range(1, n_a)))
    finish(heads - 1)
    first = lax.all_to_all(after(first, *whole[-2], *whole[-1]), "g", 0, 0)
    grad_pieces = [[some[k] for some in grad_pieces] for k in range(n_g)]
    whole = [[some[k] for some in whole] for k in range(n_g)]

    mine, theirs = group_grad(scalars, own_pieces, grad_pieces, n_a, n_c)
    qkv_grad = add_high(mine, shift(theirs, "c", 1))
    qkv_grad = qkv_grad.reshape(n_a, n_g, n_r, share, columns)
    qkv_grad = scatter_sum(scatter_sum(qkv_grad, "a", 0), "r", 1)
    last = [some[-1] for some in whole[1:]]
    second = jnp.concatenate([qkv_grad.astype(BF16), second], axis=2)
    second = lax.all_to_all(after(second, *last), "g", 0, 0)

    input_grad = input_gradient(scalars, tokens, grad_resid, gain_one[None], qkv_weight, whole)

    qkv_share = (
        second[:, :, :columns]
        .astype(F32)
        .reshape(n_g, share, heads, 3, HEAD)
        .transpose(1, 3, 0, 2, 4)
        .reshape(share, 3 * width)
    )
    shares = []
    for total in (first, second[:, :, columns:]):
        total = jnp.sum(total.astype(F32), axis=0)
        shares += [
            total[:, at * width : (at + 1) * width] for at in range(total.shape[1] // width)
        ]
    out_share = shares[0]
    up_turned_share = jnp.stack(shares[1::2], axis=1)
    up_share = (
        up_turned_share.reshape(share, wide, n_all, share)
        .transpose(0, 2, 1, 3)
        .reshape(share, hidden)
    )
    down_share = jnp.concatenate(shares[2::2], axis=0)

    place = lax.axis_index(ALL) * share
    own_gain_one = lax.dynamic_slice_in_dim(gain_one, place, share)
    own_gain_two = lax.dynamic_slice_in_dim(gain_two, place, share)
    first_share = jnp.sum(qkv_low.astype(F32) * qkv_share, axis=1) / own_gain_one
    second_share = jnp.sum(up_turned.astype(F32) * up_turned_share, axis=(1, 2)) / own_gain_two
    return (
        mixed,
        input_grad,
        qkv_share,
        out_share,
        up_share,
        down_share,
        first_share,
        second_share,
    )


def solution(mesh):
    n_scene, n_seq = mesh.devices.shape
    n_g = math.gcd(HEADS, n_seq)
    inner = Mesh(mesh.devices.reshape(n_scene // 2, 2, n_g, n_seq // n_g), ALL)
    split = P(ALL, None)
    in_specs = (split, P(("a", "c")), split, split, split, split, split, P(), P())
    out_specs = (split, split, split, split, split, split, P(ALL), P(ALL))
    return jax.shard_map(
        on_device, mesh=inner, in_specs=in_specs, out_specs=out_specs, check_vma=False
    )
```

```python
import functools
import math

import jax
import jax.numpy as jnp
from jax import lax
from jax.experimental import pallas as pl
from jax.experimental.pallas import tpu as pltpu
from jax.sharding import Mesh
from jax.sharding import PartitionSpec as P

HEADS = 12
HEAD = 64
LANES = 128
NEG_BIG = -1e30
EPS = 1e-05
SCALE = 0.125
EXP_SCALE = SCALE * math.log2(math.e)
VMEM_LIMIT = 60 * 1024 * 1024
GELU_A = math.sqrt(2.0 / math.pi)
GELU_B = 0.044715
F32 = jnp.float32
BF16 = jnp.bfloat16
ALL = ("a", "c", "g", "r")


def nt(left, right):
    return lax.dot_general(left, right, (((1,), (1,)), ((), ())), preferred_element_type=F32)


def nn(left, right):
    return lax.dot_general(left, right, (((1,), (0,)), ((), ())), preferred_element_type=F32)


def tn(left, right):
    return lax.dot_general(left, right, (((0,), (0,)), ((), ())), preferred_element_type=F32)


def three_parts(value):
    first = value.astype(BF16)
    rest = value - first.astype(F32)
    second = rest.astype(BF16)
    third = (rest - second.astype(F32)).astype(BF16)
    return first, second, third


def block_rows(rows):
    return 256 if rows % 256 == 0 else rows


def attention_forward_kernel(n_own, live_ref, *refs):
    n_pieces = len(refs) - 6
    pieces, weight = refs[:n_pieces], refs[n_pieces]
    out_ref, query_ref, key_ref, value_ref, out_scr = refs[n_pieces + 1 :]
    rows = pieces[0].shape[0]
    half = rows // 2
    lane = lax.broadcasted_iota(jnp.int32, (rows, HEAD), 1)
    slot = lax.broadcasted_iota(jnp.int32, (rows, HEAD), 0)
    bias = jnp.where(slot < live_ref[0], 0.0, NEG_BIG)
    key_extra = jnp.where(lane == 0, bias, jnp.where(lane < 4, 1.0, 0.0)).astype(BF16)
    value_extra = jnp.where(lane < 3, 1.0, 0.0).astype(BF16)
    query_extra = jnp.where(lane == 0, 1.0, 0.0).astype(BF16)
    for index in range(n_pieces):
        made = nn(pieces[index][...], weight[0]).astype(BF16)
        here = slice(index * rows, (index + 1) * rows)
        key_ref[0, here, :] = jnp.concatenate([made[:, HEAD : 2 * HEAD], key_extra], axis=1)
        value_ref[0, here, :] = jnp.concatenate([made[:, 2 * HEAD :], value_extra], axis=1)
        if index < n_own:
            query_ref[0, here, :] = jnp.concatenate([made[:, :HEAD], query_extra], axis=1)

    size = block_rows(rows * n_own)
    blocks = rows * n_own // size
    full = lax.broadcasted_iota(jnp.int32, (size, LANES), 1)
    keys = key_ref[0]
    values = value_ref[0]
    scores = nt(query_ref[0, :size], keys)
    for block in range(blocks):
        here = slice(block * size, (block + 1) * size)
        later = None
        if block + 1 < blocks:
            later = nt(query_ref[0, (block + 1) * size : (block + 2) * size], keys)
        highest = jnp.max(scores, axis=1, keepdims=True)
        weights = jnp.exp2((scores - highest) * EXP_SCALE).astype(BF16)
        summed = nn(weights, values)
        total = summed[:, HEAD : HEAD + 1]
        out_scr[here, :] = summed / total
        first, second, third = three_parts(-(highest + jnp.log2(total) * (1.0 / EXP_SCALE)))
        query_ref[0, here, :] = jnp.where(
            full == HEAD + 1,
            first,
            jnp.where(
                full == HEAD + 2, second, jnp.where(full == HEAD + 3, third, query_ref[0, here, :])
            ),
        )
        scores = later
    for index in range(n_own):
        base = index * rows
        upper = out_scr[base : base + half, :HEAD]
        lower = out_scr[base + half : base + rows, :HEAD]
        out_ref[index, 0] = jnp.concatenate([upper, lower], axis=1).astype(BF16)


def attention_forward(live, pieces, weight, n_own):
    heads = weight.shape[0]
    rows, width = pieces[0].shape
    n_keys = rows * len(pieces)
    n_queries = rows * n_own
    half = rows // 2
    per_head = lambda n: pl.BlockSpec((1, n, LANES), lambda h: (h, 0, 0))
    return pl.pallas_call(
        functools.partial(attention_forward_kernel, n_own),
        grid=(heads,),
        in_specs=[pl.BlockSpec(memory_space=pltpu.SMEM)]
        + [pl.BlockSpec((rows, width), lambda h: (0, 0), pipeline_mode=pl.Buffered(1)) for _ in pieces]
        + [pl.BlockSpec((1, width, 3 * HEAD), lambda h: (h, 0, 0))],
        out_specs=[
            pl.BlockSpec((n_own, 1, half, LANES), lambda h: (0, h, 0, 0)),
            per_head(n_queries),
            per_head(n_keys),
            per_head(n_keys),
        ],
        out_shape=[
            jax.ShapeDtypeStruct((n_own, heads, half, LANES), BF16),
            jax.ShapeDtypeStruct((heads, n_queries, LANES), BF16),
            jax.ShapeDtypeStruct((heads, n_keys, LANES), BF16),
            jax.ShapeDtypeStruct((heads, n_keys, LANES), BF16),
        ],
        scratch_shapes=[pltpu.VMEM((n_queries, LANES), F32)],
        compiler_params=pltpu.CompilerParams(
            dimension_semantics=("arbitrary",), vmem_limit_bytes=VMEM_LIMIT
        ),
        name="attention_forward",
    )(live, *pieces, weight)


def attention_backward_kernel(rows, n_own, out_ref, query_ref, key_ref, value_ref, *refs):
    grads = refs[:n_own]
    own_ref, send_ref, grad_query_ref, grad_scr, low_scr, key_scr, query_scr, acc_scr = refs[n_own:]
    half = rows // 2
    lane = lax.broadcasted_iota(jnp.int32, (rows, HEAD), 1)
    for index in range(n_own):
        packed = grads[index][0]
        grad = jnp.concatenate([packed[:, :HEAD], packed[:, HEAD:]], axis=0)
        packed_out = out_ref[index, 0]
        attended = jnp.concatenate([packed_out[:, :HEAD], packed_out[:, HEAD:]], axis=0)
        delta = jnp.sum(grad.astype(F32) * attended.astype(F32), axis=1, keepdims=True)
        first, second, third = three_parts(-delta)
        zeros = jnp.zeros_like(grad)
        extra = jnp.where(
            lane == 0, first, jnp.where(lane == 1, second, jnp.where(lane == 2, third, zeros))
        )
        here = slice(index * rows, (index + 1) * rows)
        grad_scr[here, :] = jnp.concatenate([grad, extra], axis=1)
        low_scr[here, :] = jnp.concatenate([zeros, grad], axis=1)
    key_scr[...] = key_ref[0].T

    size = block_rows(rows * n_own)
    blocks = rows * n_own // size
    keys = key_ref[0]
    values = value_ref[0]
    full = lax.broadcasted_iota(jnp.int32, (size, LANES), 1)

    def products(block):
        here = slice(block * size, (block + 1) * size)
        return nt(keys, query_ref[0, here, :]), nt(values, grad_scr[here, :])

    scores, change = products(0)
    for block in range(blocks):
        here = slice(block * size, (block + 1) * size)
        later = products(block + 1) if block + 1 < blocks else (None, None)
        weights = jnp.exp2(scores * EXP_SCALE)
        dscore = (weights * change).astype(BF16)
        query = query_ref[0, here, :]
        plain = jnp.where(full < HEAD, query * SCALE, jnp.zeros_like(query))
        terms = nn(
            jnp.concatenate([weights.astype(BF16), dscore], axis=1),
            jnp.concatenate([low_scr[here, :], plain], axis=0),
        )
        if block == 0:
            acc_scr[...] = terms
        else:
            acc_scr[...] += terms
        query_scr[here, :] = nn(key_scr[...], dscore).T * SCALE
        scores, change = later
    for index in range(n_own):
        base = index * rows
        upper = query_scr[base : base + half, :HEAD]
        lower = query_scr[base + half : base + rows, :HEAD]
        grad_query_ref[index] = jnp.concatenate([upper, lower], axis=1).astype(BF16)
        own_ref[index] = acc_scr[base : base + rows, :]
    for index in range(send_ref.shape[0]):
        base = (n_own + index) * rows
        send_ref[index] = acc_scr[base : base + rows, :].astype(BF16)


def attention_backward(out, query, key, value, grads, head):
    n_own, _, half, _ = out.shape
    rows = 2 * half
    n_queries, n_keys = query.shape[1], key.shape[1]
    n_send = n_keys // rows - n_own
    per_head = lambda n: pl.BlockSpec((1, n, LANES), lambda i: (head, 0, 0))
    stacked = lambda k, n: pl.BlockSpec((k, 1, n, LANES), lambda i: (0, head, 0, 0))
    vmem = pl.BlockSpec(memory_space=pltpu.VMEM)
    return pl.pallas_call(
        functools.partial(attention_backward_kernel, rows, n_own),
        grid=(1,),
        in_specs=[stacked(n_own, half), per_head(n_queries), per_head(n_keys), per_head(n_keys)]
        + [per_head(half) for _ in grads],
        out_specs=[vmem, vmem, vmem],
        out_shape=[
            jax.ShapeDtypeStruct((n_own, rows, LANES), F32),
            jax.ShapeDtypeStruct((n_send, rows, LANES), BF16),
            jax.ShapeDtypeStruct((n_own, half, LANES), BF16),
        ],
        scratch_shapes=[
            pltpu.VMEM((n_queries, LANES), BF16),
            pltpu.VMEM((n_queries, LANES), BF16),
            pltpu.VMEM((LANES, n_keys), BF16),
            pltpu.VMEM((n_queries, LANES), F32),
            pltpu.VMEM((n_keys, LANES), F32),
        ],
        compiler_params=pltpu.CompilerParams(
            dimension_semantics=("arbitrary",), vmem_limit_bytes=VMEM_LIMIT
        ),
        name="attention_backward",
    )(out, query, key, value, *grads)


def unpack_rows(packed):
    heads = packed.shape[0]
    return jnp.concatenate(
        [
            jnp.concatenate([packed[h, :, :HEAD], packed[h, :, HEAD:]], axis=0)
            for h in range(heads)
        ],
        axis=1,
    )


def middle_kernel(sizes, scalar_ref, *refs):
    n_g, wide, width, rows, n_a, chunks = sizes
    refs = list(refs)

    def take(count):
        taken = refs[:count]
        del refs[:count]
        return taken

    token_ref, cotangent_ref, gain_ref = take(3)
    pieces = take(n_g)
    (weight_hbm,) = take(1)
    mixed_ref, resid_ref = take(2)
    grads = take(n_g)
    grad_hbm = [take(2 * n_a) for _ in chunks]
    weight_scr, made_scr, attended_scr, in_sem, out_sem = refs
    half = rows // 2
    part = width // n_g
    heads = part // HEAD
    block = width // (2 * n_a)
    here_a, here_c = scalar_ref[3], scalar_ref[2]

    def row_block(step_a, step_c):
        at_a = here_a + step_a
        at_a = jnp.where(at_a >= n_a, at_a - n_a, at_a)
        at_c = jnp.where(here_c + step_c >= 2, 0, here_c + step_c)
        return pl.ds(pl.multiple_of((at_a * 2 + at_c) * block, block), block)

    def chunk_of(index):
        first = 0
        for number, count in enumerate(chunks):
            if index < first + count:
                return number, pl.ds((index - first) * width, width)
            first += count

    def fetch(index):
        return [
            pltpu.make_async_copy(
                weight_hbm.at[:, pl.ds(index * width, width)],
                weight_scr.at[index],
                in_sem.at[index],
            )
        ]

    def flush(index):
        number, columns = chunk_of(index)
        return [
            pltpu.make_async_copy(
                made_scr.at[index, row_block(step_a, step_c)],
                grad_hbm[number][step_c * n_a + step_a].at[:, columns],
                out_sem.at[index, step_c * n_a + step_a],
            )
            for step_c in range(2)
            for step_a in range(n_a)
        ]

    def start(copies):
        for copy in copies:
            copy.start()

    def wait(copies):
        for copy in copies:
            copy.wait()

    count = 1 + 2 * wide
    for index in [0] + [at + q for q in range(wide) for at in (1, 1 + wide)]:
        start(fetch(index))

    def places(k):
        at = scalar_ref[1] - k
        at = jnp.where(at < 0, at + n_g, at)
        return pl.ds(pl.multiple_of(at * part, part), part)

    resid = token_ref[...].astype(F32)
    for k in range(n_g):
        attended_scr[k] = unpack_rows(pieces[k][...])
    wait(fetch(0))
    for k in range(n_g):
        resid = resid + nn(attended_scr[k], weight_scr[0, places(k), :])
    gain = gain_ref[...]
    mean = jnp.mean(resid, axis=1, keepdims=True)
    centered = resid - mean
    inverse = lax.rsqrt(jnp.mean(centered * centered, axis=1, keepdims=True) + EPS)
    scaled = centered * inverse
    normed = (scaled * gain).astype(BF16)
    slot = lax.broadcasted_iota(jnp.int32, (rows, width), 0)
    grad_low = jnp.where(
        slot < scalar_ref[0], cotangent_ref[...].astype(F32), 0.0
    ).astype(BF16)
    normed_turned = normed.T
    added = None
    grad_normed = None
    for q in range(wide):
        up_at, down_at = 1 + q, 1 + wide + q
        wait(fetch(up_at))
        upper = nn(normed, weight_scr[up_at])
        wait(fetch(down_at))
        grad_active = nt(grad_low, weight_scr[down_at])
        square = upper * upper
        inner = jnp.tanh((GELU_A * upper) * (1.0 + GELU_B * square))
        onward = 0.5 * (1.0 + inner)
        active = (upper * onward).astype(BF16)
        slope = onward + (0.5 * GELU_A) * upper * (1.0 - inner * inner) * (
            1.0 + (3.0 * GELU_B) * square
        )
        grad_upper = (grad_active * slope).astype(BF16)
        more = nn(active, weight_scr[down_at])
        added = more if added is None else added + more
        made_scr[down_at] = tn(active, grad_low).astype(BF16)
        start(flush(down_at))
        made_scr[up_at] = nn(normed_turned, grad_upper).astype(BF16)
        start(flush(up_at))
        more = nt(grad_upper, weight_scr[up_at])
        grad_normed = more if grad_normed is None else grad_normed + more
    mixed_ref[...] = (resid + added).astype(BF16)
    grad_scaled = grad_normed * gain
    first = jnp.mean(grad_scaled, axis=1, keepdims=True)
    second = jnp.mean(grad_scaled * scaled, axis=1, keepdims=True)
    grad_resid = grad_low.astype(F32) + inverse * (grad_scaled - first - scaled * second)
    resid_ref[...] = grad_resid
    branch = grad_resid.astype(BF16)
    for k in range(n_g):
        grad_block = nt(branch, weight_scr[0, places(k), :])
        for h in range(heads):
            here = slice(h * HEAD, (h + 1) * HEAD)
            grads[k][h] = jnp.concatenate(
                [grad_block[:half, here], grad_block[half:, here]], axis=1
            ).astype(BF16)
    for k in range(n_g):
        made_scr[0, places(k), :] = tn(attended_scr[k], branch).astype(BF16)
    start(flush(0))
    for index in range(count):
        wait(flush(index))


def middle(scalars, tokens, cotangent, gain, pieces, weights, n_a):
    rows, width = tokens.shape
    n_g = len(pieces)
    count = weights.shape[1] // width
    wide = (count - 1) // 2
    chunks = (1 + 2 * (wide // 2), 2 * (wide - wide // 2))
    vmem = pl.BlockSpec(memory_space=pltpu.VMEM)
    anywhere = pl.BlockSpec(memory_space=pl.ANY)
    flat = [
        jax.ShapeDtypeStruct((width // (2 * n_a), chunk * width), BF16)
        for chunk in chunks
        for _ in range(2 * n_a)
    ]
    return pl.pallas_call(
        functools.partial(middle_kernel, (n_g, wide, width, rows, n_a, chunks)),
        in_specs=[pl.BlockSpec(memory_space=pltpu.SMEM)] + [vmem] * (3 + n_g) + [anywhere],
        out_specs=[vmem] * (2 + n_g) + [anywhere] * len(flat),
        out_shape=[
            jax.ShapeDtypeStruct((rows, width), BF16),
            jax.ShapeDtypeStruct((rows, width), F32),
        ]
        + [jax.ShapeDtypeStruct(piece.shape, BF16) for piece in pieces]
        + flat,
        scratch_shapes=[
            pltpu.VMEM((count, width, width), BF16),
            pltpu.VMEM((count, width, width), BF16),
            pltpu.VMEM((n_g, rows, width // n_g), BF16),
            pltpu.SemaphoreType.DMA((count,)),
            pltpu.SemaphoreType.DMA((count, 2 * n_a)),
        ],
        compiler_params=pltpu.CompilerParams(vmem_limit_bytes=VMEM_LIMIT),
        name="middle",
    )(scalars, tokens, cotangent, gain, *pieces, weights)


def combine_kernel(rows, n_terms, own_ref, query_ref, *refs):
    terms, outs = refs[:n_terms], refs[n_terms:]
    for k, out_ref in enumerate(outs):
        total = own_ref[k]
        for term in terms:
            total = total + term[k].astype(F32)
        out_ref[:rows, :] = total.astype(BF16)
        out_ref[rows:, :] = query_ref[k]


def combine(own, grad_query, terms):
    n_g, rows, _ = own.shape
    vmem = pl.BlockSpec(memory_space=pltpu.VMEM)
    shape = (rows + grad_query.shape[1], LANES)
    return pl.pallas_call(
        functools.partial(combine_kernel, rows, len(terms)),
        in_specs=[vmem] * (2 + len(terms)),
        out_specs=[vmem] * n_g,
        out_shape=[jax.ShapeDtypeStruct(shape, BF16)] * n_g,
        compiler_params=pltpu.CompilerParams(vmem_limit_bytes=VMEM_LIMIT),
        name="combine",
    )(own, grad_query, *terms)


def unpack_grads(pieces, rows):
    parts = []
    for piece in pieces:
        packed = piece[rows:, :]
        parts.append(jnp.concatenate([packed[:, :HEAD], packed[:, HEAD:]], axis=0))
        parts.append(piece[:rows, :])
    return jnp.concatenate(parts, axis=1)


def group_grad_kernel(n_g, n_a, scalar_ref, *refs):
    inputs, pieces = refs[:n_g], refs[n_g:-3]
    mine_ref, other_ref, scr = refs[-3:]
    heads = len(pieces) // n_g
    rows = inputs[0].shape[0]
    left = jnp.concatenate([ref[...] for ref in inputs], axis=0)
    right = [
        unpack_grads([ref[...] for ref in pieces[k * heads : (k + 1) * heads]], rows)
        for k in range(n_g)
    ]
    right = jnp.concatenate(right, axis=0)
    scr[...] = tn(left, right)
    block = mine_ref.shape[1]
    n_c = scr.shape[0] // (n_a * block)
    for a in range(n_a):
        mine = pl.ds(pl.multiple_of((a * n_c + scalar_ref[2]) * block, block), block)
        other = pl.ds(pl.multiple_of((a * n_c + n_c - 1 - scalar_ref[2]) * block, block), block)
        mine_ref[a] = scr[mine, :]
        other_ref[a] = scr[other, :].astype(BF16)


def group_grad(scalars, inputs, pieces, n_a, n_c):
    rows, width = inputs[0].shape
    n_g = len(pieces)
    heads = len(pieces[0])
    columns = heads * 3 * HEAD
    block = width // (n_a * n_c)
    vmem = pl.BlockSpec(memory_space=pltpu.VMEM)
    return pl.pallas_call(
        functools.partial(group_grad_kernel, n_g, n_a),
        in_specs=[pl.BlockSpec(memory_space=pltpu.SMEM)] + [vmem] * (n_g * (1 + heads)),
        out_specs=[vmem] * 2,
        out_shape=[
            jax.ShapeDtypeStruct((n_a, block, columns), F32),
            jax.ShapeDtypeStruct((n_a, block, columns), BF16),
        ],
        scratch_shapes=[pltpu.VMEM((width, columns), F32)],
        compiler_params=pltpu.CompilerParams(vmem_limit_bytes=VMEM_LIMIT),
        name="group_grad",
    )(scalars, *inputs, *(piece for some in pieces for piece in some))


def input_grad_kernel(n_g, scalar_ref, token_ref, resid_ref, gain_ref, weight_ref, *refs):
    pieces, (out_ref, scr) = refs[:-2], refs[-2:]
    heads = len(pieces) // n_g
    rows, width = token_ref.shape
    padded = scr.shape[2]
    for k in range(n_g):
        at = scalar_ref[1] - k
        at = jnp.where(at < 0, at + n_g, at)
        made = unpack_grads([ref[...] for ref in pieces[k * heads : (k + 1) * heads]], rows)
        pad = jnp.zeros((rows, padded - made.shape[1]), BF16)
        scr[at] = jnp.concatenate([made, pad], axis=1)
    grad = nt(scr[0], weight_ref[:, :padded])
    for k in range(1, n_g):
        grad = grad + nt(scr[k], weight_ref[:, k * padded : (k + 1) * padded])
    values = token_ref[...].astype(F32)
    mean = jnp.mean(values, axis=1, keepdims=True)
    centered = values - mean
    inverse = lax.rsqrt(jnp.mean(centered * centered, axis=1, keepdims=True) + EPS)
    scaled = centered * inverse
    grad_scaled = grad * gain_ref[...]
    first = jnp.mean(grad_scaled, axis=1, keepdims=True)
    second = jnp.mean(grad_scaled * scaled, axis=1, keepdims=True)
    out_ref[...] = resid_ref[...] + inverse * (grad_scaled - first - scaled * second)


def input_gradient(scalars, tokens, grad_resid, gain, weight, pieces):
    rows, width = tokens.shape
    n_g = len(pieces)
    flat = [piece for some in pieces for piece in some]
    vmem = pl.BlockSpec(memory_space=pltpu.VMEM)
    return pl.pallas_call(
        functools.partial(input_grad_kernel, n_g),
        in_specs=[pl.BlockSpec(memory_space=pltpu.SMEM)] + [vmem] * (4 + len(flat)),
        out_specs=vmem,
        out_shape=jax.ShapeDtypeStruct((rows, width), F32),
        scratch_shapes=[pltpu.VMEM((n_g, rows, weight.shape[1] // n_g), BF16)],
        compiler_params=pltpu.CompilerParams(vmem_limit_bytes=VMEM_LIMIT),
        name="input_gradient",
    )(scalars, tokens, grad_resid, gain, weight, *flat)


def norm_rows(values, gain_vector):
    mean_value = jnp.mean(values, axis=-1, keepdims=True)
    centered = values - mean_value
    variance = jnp.mean(centered * centered, axis=-1, keepdims=True)
    return centered * lax.rsqrt(variance + EPS) * gain_vector


def shift(value, axis, step):
    n = lax.axis_size(axis)
    return lax.ppermute(value, axis, [(i, (i + step) % n) for i in range(n)])


def gather(value, axis):
    n = lax.axis_size(axis)
    if n == 1:
        return value[None]
    if n == 2:
        other = shift(value, axis, 1)
        first = lax.axis_index(axis) == 0
        return jnp.stack([jnp.where(first, value, other), jnp.where(first, other, value)])
    return lax.all_gather(value, axis, axis=0)


def after(value, *others):
    return lax.optimization_barrier((value,) + others)[0]


def add_high(*terms):
    total = terms[0].astype(F32)
    for term in terms[1:]:
        total = total + term.astype(F32)
    return total


def add_low(*terms):
    return add_high(*terms).astype(BF16)


def halves(value, axis, dim):
    n = lax.axis_size(axis)
    me = lax.axis_index(axis)
    mine = lax.dynamic_index_in_dim(value, me, dim, keepdims=False)
    others = [
        lax.dynamic_index_in_dim(value, (me + j) % n, dim, keepdims=False).astype(BF16)
        for j in range(1, n)
    ]
    return mine, others


def sum_halves(mine, others, axis):
    return add_high(mine, *(shift(other, axis, j) for j, other in enumerate(others, 1)))


def scatter_sum(value, axis, dim):
    return sum_halves(*halves(value, axis, dim), axis)


def on_device(
    tokens,
    scene_tokens,
    cotangent,
    qkv_master,
    out_master,
    up_master,
    down_master,
    gain_one,
    gain_two,
):
    rows, width = tokens.shape
    hidden = up_master.shape[1]
    n_a, n_c, n_g, n_r = (lax.axis_size(axis) for axis in ALL)
    share = qkv_master.shape[0]
    wide = hidden // width
    heads = HEADS // n_g
    live_count = scene_tokens[0]

    normed_low = norm_rows(tokens.astype(F32), gain_one).astype(BF16)
    qkv_low = qkv_master.astype(BF16)
    parts = qkv_low.reshape(share, 3, n_g, heads, HEAD).transpose(2, 0, 3, 1, 4)
    parts = parts.reshape(n_g, share, heads * 3 * HEAD)
    own_pieces = [normed_low] * n_g
    for k in {1, n_g - 1}:
        own_pieces[k] = shift(normed_low, "g", -k)
    ready = [own_pieces[1], own_pieces[n_g - 1]]
    others = {(j, 0): shift(normed_low, "r", -j) for j in range(1, n_r)}
    ready += others.values()
    parts = lax.all_to_all(parts, "g", 0, 0)
    ready.append(parts)
    for k in range(2, n_g - 1):
        own_pieces[k] = shift(after(own_pieces[k - 1], *ready), "g", -1)
    for k in sorted(range(1, n_g), key=lambda k: min(k, n_g - k)):
        for j in range(1, n_r):
            others[j, k] = shift(after(own_pieces[k], *ready), "r", -j)
    pieces = own_pieces + [others[at] for at in sorted(others)]

    n_all = n_a * n_c * n_g * n_r
    up_turned = (
        up_master.astype(BF16)
        .reshape(share, n_all, wide, share)
        .transpose(0, 2, 1, 3)
        .reshape(share, hidden)
    )
    down_turned = down_master.astype(BF16).reshape(wide, share, width)
    packed = jnp.concatenate([out_master.astype(BF16), up_turned, *down_turned], axis=1)
    weights = lax.all_gather(packed, ALL, axis=0, tiled=True)

    parts = gather(gather(gather(after(parts, *ready), "r"), "c"), "a")
    parts = parts.reshape(n_a, n_c, n_r, n_g, share, heads, 3 * HEAD)
    group_weight = parts.transpose(5, 0, 1, 3, 2, 4, 6).reshape(heads, width, 3 * HEAD)

    scalars = jnp.stack(
        [live_count, lax.axis_index("g"), lax.axis_index("c"), lax.axis_index("a")]
    )
    out, query, key, value = attention_forward(scene_tokens, pieces, group_weight, n_g)
    back = [out[0]] + [shift(out[k], "g", k) for k in range(1, n_g)]
    made = middle(scalars, tokens, cotangent, gain_two[None], back, weights, n_a)
    mixed, grad_resid, sends = made[0], made[1], made[2 : 2 + n_g]
    grad_blocks = [made[2 + n_g : 2 + n_g + n_a * n_c], made[2 + n_g + n_a * n_c :]]

    come = [[shift(block, "c", 1) for block in some[n_a:]] for some in grad_blocks]

    columns = heads * 3 * HEAD
    padded = -(-columns // LANES) * LANES
    turned = qkv_low.reshape(share, 3, n_g, heads, HEAD).transpose(0, 2, 3, 1, 4)
    turned = turned.reshape(share, n_g, columns)
    qkv_weight = jnp.pad(turned, ((0, 0), (0, 0), (0, padded - columns)))
    qkv_weight = after(qkv_weight.reshape(share, n_g * padded), *ready)
    qkv_weight = lax.all_gather(qkv_weight, ALL, axis=0, tiled=True)

    grads = [sends[0]] + [shift(sends[k], "g", -k) for k in range(1, n_g)]
    made = []
    grad_pieces = []
    whole = []

    def finish(head):
        own, across, grad_query = made[head]
        own = after(own, made[min(head + 1, heads - 1)][0])
        if head >= 2:
            own = after(own, *whole[head - 2])
        done = combine(own, grad_query, across)
        grad_pieces.append(done)
        whole.append([done[0]] + [shift(done[k], "g", k) for k in range(1, n_g)])

    for head in range(heads):
        gate = [made[-1][0]] if head == 1 else []
        if head == 0:
            come = [[after(block, *grads) for block in some] for some in come]
            far = [
                [add_low(*pair) for pair in zip(some[1:n_a], there[1:])]
                for some, there in zip(grad_blocks, come)
            ]
            gate = far[0] + far[1]
            far[0] = [shift(block, "a", k) for k, block in enumerate(far[0], 1)]
        if head >= 2:
            finish(head - 2)
            gate = [*grad_pieces[head - 2], qkv_weight]
        gated = ([after(grads[0], *gate)] if gate else grads[:1]) + grads[1:]
        own, across, grad_query = attention_backward(out, query, key, value, gated, head)
        across = [
            shift(across[(j - 1) * n_g : j * n_g] if n_r > 2 else across, "r", j)
            for j in range(1, n_r)
        ]
        made.append((own, across, grad_query))
    made[-2] = (after(made[-2][0], *whole[-1]),) + made[-2][1:]
    finish(heads - 2)
    far[0] = [after(block, *grad_pieces[-1]) for block in far[0]]
    first = add_high(grad_blocks[0][0], come[0][0], *far[0])
    first, send = halves(first.reshape(n_g, n_r, share, -1), "r", 1)
    far[1] = [after(block, *far[0]) for block in far[1]]
    made[-1] = (after(made[-1][0], *send),) + made[-1][1:]
    finish(heads - 1)
    send = [shift(after(block, *made[-1][1]), "r", j) for j, block in enumerate(send, 1)]
    far[1] = [shift(block, "a", k) for k, block in enumerate(far[1], 1)]
    second = add_high(grad_blocks[1][0], come[1][0], *far[1]).reshape(n_g, n_r, share, -1)
    second = scatter_sum(second, "r", 1).astype(BF16)
    grad_pieces = [[some[k] for some in grad_pieces] for k in range(n_g)]
    whole = [[some[k] for some in whole] for k in range(n_g)]

    grad_pieces[0][0] = after(grad_pieces[0][0], *(some[-2] for some in whole))
    mine, theirs = group_grad(scalars, own_pieces, grad_pieces, n_a, n_c)
    theirs = after(theirs, *(some[-1] for some in whole), *send)
    first = lax.all_to_all(add_low(first, *send), "g", 0, 0)
    qkv_grad = add_high(mine, shift(theirs, "c", 1))
    qkv_grad = qkv_grad.reshape(n_a, n_g, n_r, share, columns)
    qkv_grad = scatter_sum(after(scatter_sum(qkv_grad, "a", 0), first), "r", 1)
    second = jnp.concatenate([qkv_grad.astype(BF16), second], axis=2)
    second = lax.all_to_all(after(second, first), "g", 0, 0)
    input_grad = input_gradient(scalars, tokens, grad_resid, gain_one[None], qkv_weight, whole)

    first = jnp.sum(first.astype(F32), axis=0)
    out_share = first[:, :width]
    up_share = first[:, width:]
    second_share = jnp.sum(up_turned.astype(F32) * up_share, axis=1)
    up_share = (
        up_share.reshape(share, wide, n_all, share).transpose(0, 2, 1, 3).reshape(share, hidden)
    )
    qkv_share = second[:, :, :columns].astype(F32)
    first_share = jnp.sum(turned.swapaxes(0, 1).astype(F32) * qkv_share, axis=(0, 2))
    qkv_share = (
        qkv_share.reshape(n_g, share, heads, 3, HEAD)
        .transpose(1, 3, 0, 2, 4)
        .reshape(share, 3 * width)
    )
    down_share = jnp.sum(second[:, :, columns:].astype(F32), axis=0)
    down_share = (
        down_share.reshape(share, wide, width).transpose(1, 0, 2).reshape(wide * share, width)
    )

    place = lax.axis_index(ALL) * share
    own_gain_one = lax.dynamic_slice_in_dim(gain_one, place, share)
    own_gain_two = lax.dynamic_slice_in_dim(gain_two, place, share)
    first_share = first_share / own_gain_one
    second_share = second_share / own_gain_two
    return (
        mixed,
        input_grad,
        qkv_share,
        out_share,
        up_share,
        down_share,
        first_share,
        second_share,
    )


def solution(mesh):
    n_scene, n_seq = mesh.devices.shape
    n_g = math.gcd(HEADS, n_seq)
    inner = Mesh(mesh.devices.reshape(n_scene // 2, 2, n_g, n_seq // n_g), ALL)
    split = P(ALL, None)
    in_specs = (split, P(("a", "c")), split, split, split, split, split, P(), P())
    out_specs = (split, split, split, split, split, split, P(ALL), P(ALL))
    return jax.shard_map(
        on_device, mesh=inner, in_specs=in_specs, out_specs=out_specs, check_vma=False
    )
```

```python
import functools
import math

import jax
import jax.numpy as jnp
from jax import lax
from jax.experimental import pallas as pl
from jax.experimental.pallas import tpu as pltpu
from jax.sharding import Mesh
from jax.sharding import PartitionSpec as P

HEADS = 12
HEAD = 64
LANES = 128
NEG_BIG = -1e30
EPS = 1e-05
SCALE = 0.125
EXP_SCALE = SCALE * math.log2(math.e)
VMEM_LIMIT = 60 * 1024 * 1024
GELU_A = math.sqrt(2.0 / math.pi)
GELU_B = 0.044715
F32 = jnp.float32
BF16 = jnp.bfloat16
ALL = ("a", "c", "g", "r")


def nt(left, right):
    return lax.dot_general(left, right, (((1,), (1,)), ((), ())), preferred_element_type=F32)


def nn(left, right):
    return lax.dot_general(left, right, (((1,), (0,)), ((), ())), preferred_element_type=F32)


def tn(left, right):
    return lax.dot_general(left, right, (((0,), (0,)), ((), ())), preferred_element_type=F32)


def three_parts(value):
    first = value.astype(BF16)
    rest = value - first.astype(F32)
    second = rest.astype(BF16)
    third = (rest - second.astype(F32)).astype(BF16)
    return first, second, third


def block_rows(rows):
    return 256 if rows % 256 == 0 else rows


def attention_forward_kernel(n_own, live_ref, *refs):
    n_pieces = len(refs) - 6
    pieces, weight = refs[:n_pieces], refs[n_pieces]
    out_ref, query_ref, key_ref, value_ref, out_scr = refs[n_pieces + 1 :]
    rows = pieces[0].shape[0]
    half = rows // 2
    lane = lax.broadcasted_iota(jnp.int32, (rows, HEAD), 1)
    slot = lax.broadcasted_iota(jnp.int32, (rows, HEAD), 0)
    bias = jnp.where(slot < live_ref[0], 0.0, NEG_BIG)
    key_extra = jnp.where(lane == 0, bias, jnp.where(lane < 4, 1.0, 0.0)).astype(BF16)
    value_extra = jnp.where(lane < 3, 1.0, 0.0).astype(BF16)
    query_extra = jnp.where(lane == 0, 1.0, 0.0).astype(BF16)
    for index in range(n_pieces):
        made = nn(pieces[index][...], weight[0]).astype(BF16)
        here = slice(index * rows, (index + 1) * rows)
        key_ref[0, here, :] = jnp.concatenate([made[:, HEAD : 2 * HEAD], key_extra], axis=1)
        value_ref[0, here, :] = jnp.concatenate([made[:, 2 * HEAD :], value_extra], axis=1)
        if index < n_own:
            query_ref[0, here, :] = jnp.concatenate([made[:, :HEAD], query_extra], axis=1)

    size = block_rows(rows * n_own)
    blocks = rows * n_own // size
    full = lax.broadcasted_iota(jnp.int32, (size, LANES), 1)
    keys = key_ref[0]
    values = value_ref[0]
    scores = nt(query_ref[0, :size], keys)
    for block in range(blocks):
        here = slice(block * size, (block + 1) * size)
        later = None
        if block + 1 < blocks:
            later = nt(query_ref[0, (block + 1) * size : (block + 2) * size], keys)
        highest = jnp.max(scores, axis=1, keepdims=True)
        weights = jnp.exp2((scores - highest) * EXP_SCALE).astype(BF16)
        summed = nn(weights, values)
        total = summed[:, HEAD : HEAD + 1]
        out_scr[here, :] = summed / total
        first, second, third = three_parts(-(highest + jnp.log2(total) * (1.0 / EXP_SCALE)))
        query_ref[0, here, :] = jnp.where(
            full == HEAD + 1,
            first,
            jnp.where(
                full == HEAD + 2, second, jnp.where(full == HEAD + 3, third, query_ref[0, here, :])
            ),
        )
        scores = later
    for index in range(n_own):
        base = index * rows
        upper = out_scr[base : base + half, :HEAD]
        lower = out_scr[base + half : base + rows, :HEAD]
        out_ref[index, 0] = jnp.concatenate([upper, lower], axis=1).astype(BF16)


def attention_forward(live, pieces, weight, n_own):
    heads = weight.shape[0]
    rows, width = pieces[0].shape
    n_keys = rows * len(pieces)
    n_queries = rows * n_own
    half = rows // 2
    per_head = lambda n: pl.BlockSpec((1, n, LANES), lambda h: (h, 0, 0))
    return pl.pallas_call(
        functools.partial(attention_forward_kernel, n_own),
        grid=(heads,),
        in_specs=[pl.BlockSpec(memory_space=pltpu.SMEM)]
        + [pl.BlockSpec((rows, width), lambda h: (0, 0), pipeline_mode=pl.Buffered(1)) for _ in pieces]
        + [pl.BlockSpec((1, width, 3 * HEAD), lambda h: (h, 0, 0))],
        out_specs=[
            pl.BlockSpec((n_own, 1, half, LANES), lambda h: (0, h, 0, 0)),
            per_head(n_queries),
            per_head(n_keys),
            per_head(n_keys),
        ],
        out_shape=[
            jax.ShapeDtypeStruct((n_own, heads, half, LANES), BF16),
            jax.ShapeDtypeStruct((heads, n_queries, LANES), BF16),
            jax.ShapeDtypeStruct((heads, n_keys, LANES), BF16),
            jax.ShapeDtypeStruct((heads, n_keys, LANES), BF16),
        ],
        scratch_shapes=[pltpu.VMEM((n_queries, LANES), F32)],
        compiler_params=pltpu.CompilerParams(
            dimension_semantics=("arbitrary",), vmem_limit_bytes=VMEM_LIMIT
        ),
        name="attention_forward",
    )(live, *pieces, weight)


def attention_backward_kernel(rows, n_own, out_ref, query_ref, key_ref, value_ref, *refs):
    grads = refs[:n_own]
    own_ref, send_ref, grad_query_ref, grad_scr, low_scr, key_scr, query_scr, acc_scr = refs[n_own:]
    half = rows // 2
    lane = lax.broadcasted_iota(jnp.int32, (rows, HEAD), 1)
    for index in range(n_own):
        packed = grads[index][...]
        grad = jnp.concatenate([packed[:, :HEAD], packed[:, HEAD:]], axis=0)
        packed_out = out_ref[index, 0]
        attended = jnp.concatenate([packed_out[:, :HEAD], packed_out[:, HEAD:]], axis=0)
        delta = jnp.sum(grad.astype(F32) * attended.astype(F32), axis=1, keepdims=True)
        first, second, third = three_parts(-delta)
        zeros = jnp.zeros_like(grad)
        extra = jnp.where(
            lane == 0, first, jnp.where(lane == 1, second, jnp.where(lane == 2, third, zeros))
        )
        here = slice(index * rows, (index + 1) * rows)
        grad_scr[here, :] = jnp.concatenate([grad, extra], axis=1)
        low_scr[here, :] = jnp.concatenate([zeros, grad], axis=1)
    key_scr[...] = key_ref[0].T

    size = block_rows(rows * n_own)
    blocks = rows * n_own // size
    keys = key_ref[0]
    values = value_ref[0]
    full = lax.broadcasted_iota(jnp.int32, (size, LANES), 1)

    def products(block):
        here = slice(block * size, (block + 1) * size)
        return nt(keys, query_ref[0, here, :]), nt(values, grad_scr[here, :])

    scores, change = products(0)
    for block in range(blocks):
        here = slice(block * size, (block + 1) * size)
        later = products(block + 1) if block + 1 < blocks else (None, None)
        weights = jnp.exp2(scores * EXP_SCALE)
        dscore = (weights * change).astype(BF16)
        query = query_ref[0, here, :]
        plain = jnp.where(full < HEAD, query * SCALE, jnp.zeros_like(query))
        terms = nn(
            jnp.concatenate([weights.astype(BF16), dscore], axis=1),
            jnp.concatenate([low_scr[here, :], plain], axis=0),
        )
        if block == 0:
            acc_scr[...] = terms
        else:
            acc_scr[...] += terms
        query_scr[here, :] = nn(key_scr[...], dscore).T * SCALE
        scores, change = later
    for index in range(n_own):
        base = index * rows
        upper = query_scr[base : base + half, :HEAD]
        lower = query_scr[base + half : base + rows, :HEAD]
        grad_query_ref[index] = jnp.concatenate([upper, lower], axis=1).astype(BF16)
        own_ref[index] = acc_scr[base : base + rows, :]
    for index in range(send_ref.shape[0]):
        base = (n_own + index) * rows
        send_ref[index] = acc_scr[base : base + rows, :].astype(BF16)


def attention_backward(out, query, key, value, grads, head):
    n_own, _, half, _ = out.shape
    rows = 2 * half
    n_queries, n_keys = query.shape[1], key.shape[1]
    n_send = n_keys // rows - n_own
    per_head = lambda n: pl.BlockSpec((1, n, LANES), lambda i: (head, 0, 0))
    stacked = lambda k, n: pl.BlockSpec((k, 1, n, LANES), lambda i: (0, head, 0, 0))
    vmem = pl.BlockSpec(memory_space=pltpu.VMEM)
    return pl.pallas_call(
        functools.partial(attention_backward_kernel, rows, n_own),
        grid=(1,),
        in_specs=[stacked(n_own, half), per_head(n_queries), per_head(n_keys), per_head(n_keys)]
        + [
            pl.BlockSpec((None, half, LANES), lambda i: (head - 1, 0, 0)) if head else vmem
            for _ in grads
        ],
        out_specs=[vmem, vmem, vmem],
        out_shape=[
            jax.ShapeDtypeStruct((n_own, rows, LANES), F32),
            jax.ShapeDtypeStruct((n_send, rows, LANES), BF16),
            jax.ShapeDtypeStruct((n_own, half, LANES), BF16),
        ],
        scratch_shapes=[
            pltpu.VMEM((n_queries, LANES), BF16),
            pltpu.VMEM((n_queries, LANES), BF16),
            pltpu.VMEM((LANES, n_keys), BF16),
            pltpu.VMEM((n_queries, LANES), F32),
            pltpu.VMEM((n_keys, LANES), F32),
        ],
        compiler_params=pltpu.CompilerParams(
            dimension_semantics=("arbitrary",), vmem_limit_bytes=VMEM_LIMIT
        ),
        name="attention_backward",
    )(out, query, key, value, *grads)


def unpack_rows(packed):
    heads = packed.shape[0]
    return jnp.concatenate(
        [
            jnp.concatenate([packed[h, :, :HEAD], packed[h, :, HEAD:]], axis=0)
            for h in range(heads)
        ],
        axis=1,
    )


def middle_kernel(sizes, scalar_ref, *refs):
    n_g, wide, width, rows, n_a, chunks = sizes
    refs = list(refs)
    part = width // n_g
    heads = part // HEAD

    def take(count):
        taken = refs[:count]
        del refs[:count]
        return taken

    token_ref, cotangent_ref, gain_ref = take(3)
    pieces = take(n_g)
    (weight_hbm,) = take(1)
    mixed_ref, resid_ref = take(2)
    grads = take(2 * n_g)
    grad_hbm = [take(2 * n_a) for _ in chunks]
    weight_scr, made_scr, attended_scr, in_sem, out_sem = refs
    half = rows // 2
    block = width // (2 * n_a)
    here_a, here_c = scalar_ref[3], scalar_ref[2]

    def row_block(step_a, step_c):
        at_a = here_a + step_a
        at_a = jnp.where(at_a >= n_a, at_a - n_a, at_a)
        at_c = jnp.where(here_c + step_c >= 2, 0, here_c + step_c)
        return pl.ds(pl.multiple_of((at_a * 2 + at_c) * block, block), block)

    def chunk_of(index):
        first = 0
        for number, count in enumerate(chunks):
            if index < first + count:
                return number, pl.ds((index - first) * width, width)
            first += count

    def fetch(index):
        return [
            pltpu.make_async_copy(
                weight_hbm.at[:, pl.ds(index * width, width)],
                weight_scr.at[index],
                in_sem.at[index],
            )
        ]

    def flush(index):
        number, columns = chunk_of(index)
        return [
            pltpu.make_async_copy(
                made_scr.at[index, row_block(step_a, step_c)],
                grad_hbm[number][step_c * n_a + step_a].at[:, columns],
                out_sem.at[index, step_c * n_a + step_a],
            )
            for step_c in range(2)
            for step_a in range(n_a)
        ]

    def start(copies):
        for copy in copies:
            copy.start()

    def wait(copies):
        for copy in copies:
            copy.wait()

    count = 1 + 2 * wide
    for index in [0] + [at + q for q in range(wide) for at in (1, 1 + wide)]:
        start(fetch(index))

    def places(k):
        at = scalar_ref[1] - k
        at = jnp.where(at < 0, at + n_g, at)
        return pl.ds(pl.multiple_of(at * part, part), part)

    resid = token_ref[...].astype(F32)
    for k in range(n_g):
        attended_scr[k] = unpack_rows(pieces[k][...])
    wait(fetch(0))
    for k in range(n_g):
        resid = resid + nn(attended_scr[k], weight_scr[0, places(k), :])
    gain = gain_ref[...]
    mean = jnp.mean(resid, axis=1, keepdims=True)
    centered = resid - mean
    inverse = lax.rsqrt(jnp.mean(centered * centered, axis=1, keepdims=True) + EPS)
    scaled = centered * inverse
    normed = (scaled * gain).astype(BF16)
    slot = lax.broadcasted_iota(jnp.int32, (rows, width), 0)
    grad_low = jnp.where(
        slot < scalar_ref[0], cotangent_ref[...].astype(F32), 0.0
    ).astype(BF16)
    normed_turned = normed.T
    added = None
    grad_normed = None
    for q in range(wide):
        up_at, down_at = 1 + q, 1 + wide + q
        wait(fetch(up_at))
        upper = nn(normed, weight_scr[up_at])
        wait(fetch(down_at))
        grad_active = nt(grad_low, weight_scr[down_at])
        square = upper * upper
        inner = jnp.tanh((GELU_A * upper) * (1.0 + GELU_B * square))
        onward = 0.5 * (1.0 + inner)
        active = (upper * onward).astype(BF16)
        slope = onward + (0.5 * GELU_A) * upper * (1.0 - inner * inner) * (
            1.0 + (3.0 * GELU_B) * square
        )
        grad_upper = (grad_active * slope).astype(BF16)
        more = nn(active, weight_scr[down_at])
        added = more if added is None else added + more
        made_scr[down_at] = tn(active, grad_low).astype(BF16)
        start(flush(down_at))
        made_scr[up_at] = nn(normed_turned, grad_upper).astype(BF16)
        start(flush(up_at))
        more = nt(grad_upper, weight_scr[up_at])
        grad_normed = more if grad_normed is None else grad_normed + more
    mixed_ref[...] = (resid + added).astype(BF16)
    grad_scaled = grad_normed * gain
    first = jnp.mean(grad_scaled, axis=1, keepdims=True)
    second = jnp.mean(grad_scaled * scaled, axis=1, keepdims=True)
    grad_resid = grad_low.astype(F32) + inverse * (grad_scaled - first - scaled * second)
    resid_ref[...] = grad_resid
    branch = grad_resid.astype(BF16)
    for k in range(n_g):
        grad_block = nt(branch, weight_scr[0, places(k), :])
        for h in range(heads):
            here = slice(h * HEAD, (h + 1) * HEAD)
            packed = jnp.concatenate([grad_block[:half, here], grad_block[half:, here]], axis=1)
            if h == 0:
                grads[k][...] = packed.astype(BF16)
            else:
                grads[n_g + k][h - 1] = packed.astype(BF16)
    for k in range(n_g):
        made_scr[0, places(k), :] = tn(attended_scr[k], branch).astype(BF16)
    start(flush(0))
    for index in range(count):
        wait(flush(index))


def middle(scalars, tokens, cotangent, gain, pieces, weights, n_a):
    rows, width = tokens.shape
    n_g = len(pieces)
    heads, half, _ = pieces[0].shape
    count = weights.shape[1] // width
    wide = (count - 1) // 2
    chunks = (1 + 2 * (wide // 2), 2 * (wide - wide // 2))
    vmem = pl.BlockSpec(memory_space=pltpu.VMEM)
    anywhere = pl.BlockSpec(memory_space=pl.ANY)
    flat = [
        jax.ShapeDtypeStruct((width // (2 * n_a), chunk * width), BF16)
        for chunk in chunks
        for _ in range(2 * n_a)
    ]
    return pl.pallas_call(
        functools.partial(middle_kernel, (n_g, wide, width, rows, n_a, chunks)),
        in_specs=[pl.BlockSpec(memory_space=pltpu.SMEM)] + [vmem] * (3 + n_g) + [anywhere],
        out_specs=[vmem] * (2 + 2 * n_g) + [anywhere] * len(flat),
        out_shape=[
            jax.ShapeDtypeStruct((rows, width), BF16),
            jax.ShapeDtypeStruct((rows, width), F32),
        ]
        + [jax.ShapeDtypeStruct((half, LANES), BF16)] * n_g
        + [jax.ShapeDtypeStruct((heads - 1, half, LANES), BF16)] * n_g
        + flat,
        scratch_shapes=[
            pltpu.VMEM((count, width, width), BF16),
            pltpu.VMEM((count, width, width), BF16),
            pltpu.VMEM((n_g, rows, width // n_g), BF16),
            pltpu.SemaphoreType.DMA((count,)),
            pltpu.SemaphoreType.DMA((count, 2 * n_a)),
        ],
        compiler_params=pltpu.CompilerParams(vmem_limit_bytes=VMEM_LIMIT),
        name="middle",
    )(scalars, tokens, cotangent, gain, *pieces, weights)


def combine_kernel(rows, n_terms, own_ref, query_ref, *refs):
    terms, outs = refs[:n_terms], refs[n_terms:]
    for k, out_ref in enumerate(outs):
        total = own_ref[k]
        for term in terms:
            total = total + term[k].astype(F32)
        out_ref[:rows, :] = total.astype(BF16)
        out_ref[rows:, :] = query_ref[k]


def combine(own, grad_query, terms):
    n_g, rows, _ = own.shape
    vmem = pl.BlockSpec(memory_space=pltpu.VMEM)
    shape = (rows + grad_query.shape[1], LANES)
    return pl.pallas_call(
        functools.partial(combine_kernel, rows, len(terms)),
        in_specs=[vmem] * (2 + len(terms)),
        out_specs=[vmem] * n_g,
        out_shape=[jax.ShapeDtypeStruct(shape, BF16)] * n_g,
        compiler_params=pltpu.CompilerParams(vmem_limit_bytes=VMEM_LIMIT),
        name="combine",
    )(own, grad_query, *terms)


def unpack_grads(pieces, rows):
    parts = []
    for piece in pieces:
        packed = piece[rows:, :]
        parts.append(jnp.concatenate([packed[:, :HEAD], packed[:, HEAD:]], axis=0))
        parts.append(piece[:rows, :])
    return jnp.concatenate(parts, axis=1)


def group_grad_kernel(n_g, n_a, scalar_ref, *refs):
    inputs, pieces = refs[:n_g], refs[n_g:-3]
    mine_ref, other_ref, scr = refs[-3:]
    heads = len(pieces) // n_g
    rows = inputs[0].shape[0]
    left = jnp.concatenate([ref[...] for ref in inputs], axis=0)
    right = [
        unpack_grads([ref[...] for ref in pieces[k * heads : (k + 1) * heads]], rows)
        for k in range(n_g)
    ]
    right = jnp.concatenate(right, axis=0)
    scr[...] = tn(left, right)
    block = mine_ref.shape[1]
    n_c = scr.shape[0] // (n_a * block)
    for a in range(n_a):
        mine = pl.ds(pl.multiple_of((a * n_c + scalar_ref[2]) * block, block), block)
        other = pl.ds(pl.multiple_of((a * n_c + n_c - 1 - scalar_ref[2]) * block, block), block)
        mine_ref[a] = scr[mine, :]
        other_ref[a] = scr[other, :].astype(BF16)


def group_grad(scalars, inputs, pieces, n_a, n_c):
    rows, width = inputs[0].shape
    n_g = len(pieces)
    heads = len(pieces[0])
    columns = heads * 3 * HEAD
    block = width // (n_a * n_c)
    vmem = pl.BlockSpec(memory_space=pltpu.VMEM)
    return pl.pallas_call(
        functools.partial(group_grad_kernel, n_g, n_a),
        in_specs=[pl.BlockSpec(memory_space=pltpu.SMEM)] + [vmem] * (n_g * (1 + heads)),
        out_specs=[vmem] * 2,
        out_shape=[
            jax.ShapeDtypeStruct((n_a, block, columns), F32),
            jax.ShapeDtypeStruct((n_a, block, columns), BF16),
        ],
        scratch_shapes=[pltpu.VMEM((width, columns), F32)],
        compiler_params=pltpu.CompilerParams(vmem_limit_bytes=VMEM_LIMIT),
        name="group_grad",
    )(scalars, *inputs, *(piece for some in pieces for piece in some))


def input_grad_kernel(n_g, scalar_ref, token_ref, resid_ref, gain_ref, weight_ref, *refs):
    pieces, (out_ref, scr) = refs[:-2], refs[-2:]
    heads = len(pieces) // n_g
    rows, width = token_ref.shape
    padded = scr.shape[2]
    for k in range(n_g):
        at = scalar_ref[1] - k
        at = jnp.where(at < 0, at + n_g, at)
        made = unpack_grads([ref[...] for ref in pieces[k * heads : (k + 1) * heads]], rows)
        pad = jnp.zeros((rows, padded - made.shape[1]), BF16)
        scr[at] = jnp.concatenate([made, pad], axis=1)
    grad = nt(scr[0], weight_ref[:, :padded])
    for k in range(1, n_g):
        grad = grad + nt(scr[k], weight_ref[:, k * padded : (k + 1) * padded])
    values = token_ref[...].astype(F32)
    mean = jnp.mean(values, axis=1, keepdims=True)
    centered = values - mean
    inverse = lax.rsqrt(jnp.mean(centered * centered, axis=1, keepdims=True) + EPS)
    scaled = centered * inverse
    grad_scaled = grad * gain_ref[...]
    first = jnp.mean(grad_scaled, axis=1, keepdims=True)
    second = jnp.mean(grad_scaled * scaled, axis=1, keepdims=True)
    out_ref[...] = resid_ref[...] + inverse * (grad_scaled - first - scaled * second)


def input_gradient(scalars, tokens, grad_resid, gain, weight, pieces):
    rows, width = tokens.shape
    n_g = len(pieces)
    flat = [piece for some in pieces for piece in some]
    vmem = pl.BlockSpec(memory_space=pltpu.VMEM)
    return pl.pallas_call(
        functools.partial(input_grad_kernel, n_g),
        in_specs=[pl.BlockSpec(memory_space=pltpu.SMEM)] + [vmem] * (4 + len(flat)),
        out_specs=vmem,
        out_shape=jax.ShapeDtypeStruct((rows, width), F32),
        scratch_shapes=[pltpu.VMEM((n_g, rows, weight.shape[1] // n_g), BF16)],
        compiler_params=pltpu.CompilerParams(vmem_limit_bytes=VMEM_LIMIT),
        name="input_gradient",
    )(scalars, tokens, grad_resid, gain, weight, *flat)


def share_kernel(wide, got_ref, weight_ref, gain_ref, down_ref, qkv_ref, norm_ref):
    n_g, share, columns = weight_ref.shape
    heads = columns // (3 * HEAD)
    width = n_g * heads * HEAD
    for q in range(wide):
        here = slice(q * width, (q + 1) * width)
        total = got_ref[0, :, here].astype(F32)
        for g in range(1, n_g):
            total = total + got_ref[g, :, here].astype(F32)
        down_ref[q] = total
    norm = jnp.zeros((share, 1), F32)
    for g in range(n_g):
        made = got_ref[g, :, wide * width :].astype(F32)
        norm = norm + jnp.sum(made * weight_ref[g].astype(F32), axis=1, keepdims=True)
        for h in range(heads):
            for part in range(3):
                start = part * width + (g * heads + h) * HEAD
                at = (h * 3 + part) * HEAD
                qkv_ref[:, start : start + HEAD] = made[:, at : at + HEAD]
    norm_ref[...] = norm / gain_ref[...]


def last_shares(got, weight, gain):
    n_g, share, columns = weight.shape
    width = n_g * columns // 3
    wide = (got.shape[2] - columns) // width
    vmem = pl.BlockSpec(memory_space=pltpu.VMEM)
    return pl.pallas_call(
        functools.partial(share_kernel, wide),
        in_specs=[vmem] * 3,
        out_specs=[vmem] * 3,
        out_shape=[
            jax.ShapeDtypeStruct((wide, share, width), F32),
            jax.ShapeDtypeStruct((share, 3 * width), F32),
            jax.ShapeDtypeStruct((share, 1), F32),
        ],
        compiler_params=pltpu.CompilerParams(vmem_limit_bytes=VMEM_LIMIT),
        name="last_shares",
    )(got, weight, gain)


def norm_rows(values, gain_vector):
    mean_value = jnp.mean(values, axis=-1, keepdims=True)
    centered = values - mean_value
    variance = jnp.mean(centered * centered, axis=-1, keepdims=True)
    return centered * lax.rsqrt(variance + EPS) * gain_vector


def shift(value, axis, step):
    n = lax.axis_size(axis)
    return lax.ppermute(value, axis, [(i, (i + step) % n) for i in range(n)])


def gather(value, axis):
    n = lax.axis_size(axis)
    if n == 1:
        return value[None]
    if n == 2:
        other = shift(value, axis, 1)
        first = lax.axis_index(axis) == 0
        return jnp.stack([jnp.where(first, value, other), jnp.where(first, other, value)])
    return lax.all_gather(value, axis, axis=0)


def after(value, *others):
    return lax.optimization_barrier((value,) + others)[0]


def add_high(*terms):
    total = terms[0].astype(F32)
    for term in terms[1:]:
        total = total + term.astype(F32)
    return total


def add_low(*terms):
    return add_high(*terms).astype(BF16)


def halves(value, axis, dim):
    n = lax.axis_size(axis)
    me = lax.axis_index(axis)
    mine = lax.dynamic_index_in_dim(value, me, dim, keepdims=False)
    others = [
        lax.dynamic_index_in_dim(value, (me + j) % n, dim, keepdims=False).astype(BF16)
        for j in range(1, n)
    ]
    return mine, others


def sum_halves(mine, others, axis):
    return add_high(mine, *(shift(other, axis, j) for j, other in enumerate(others, 1)))


def scatter_sum(value, axis, dim):
    return sum_halves(*halves(value, axis, dim), axis)


def on_device(
    tokens,
    scene_tokens,
    cotangent,
    qkv_master,
    out_master,
    up_master,
    down_master,
    gain_one,
    gain_two,
):
    rows, width = tokens.shape
    hidden = up_master.shape[1]
    n_a, n_c, n_g, n_r = (lax.axis_size(axis) for axis in ALL)
    share = qkv_master.shape[0]
    wide = hidden // width
    heads = HEADS // n_g
    live_count = scene_tokens[0]

    normed_low = norm_rows(tokens.astype(F32), gain_one).astype(BF16)
    qkv_low = qkv_master.astype(BF16)
    parts = qkv_low.reshape(share, 3, n_g, heads, HEAD).transpose(2, 0, 3, 1, 4)
    parts = parts.reshape(n_g, share, heads * 3 * HEAD)
    own_pieces = [normed_low] * n_g
    for k in {1, n_g - 1}:
        own_pieces[k] = shift(normed_low, "g", -k)
    ready = [own_pieces[1], own_pieces[n_g - 1]]
    others = {(j, 0): shift(normed_low, "r", -j) for j in range(1, n_r)}
    ready += others.values()
    parts = lax.all_to_all(parts, "g", 0, 0)
    ready.append(parts)
    for k in range(2, n_g - 1):
        own_pieces[k] = shift(after(own_pieces[k - 1], *ready), "g", -1)
    for k in sorted(range(1, n_g), key=lambda k: min(k, n_g - k)):
        for j in range(1, n_r):
            others[j, k] = shift(after(own_pieces[k], *ready), "r", -j)
    pieces = own_pieces + [others[at] for at in sorted(others)]

    n_all = n_a * n_c * n_g * n_r
    up_turned = (
        up_master.astype(BF16)
        .reshape(share, n_all, wide, share)
        .transpose(0, 2, 1, 3)
        .reshape(share, hidden)
    )
    down_turned = down_master.astype(BF16).reshape(wide, share, width)
    packed = jnp.concatenate([out_master.astype(BF16), up_turned, *down_turned], axis=1)
    weights = lax.all_gather(packed, ALL, axis=0, tiled=True)

    parts = gather(gather(gather(after(parts, *ready), "r"), "c"), "a")
    parts = parts.reshape(n_a, n_c, n_r, n_g, share, heads, 3 * HEAD)
    group_weight = parts.transpose(5, 0, 1, 3, 2, 4, 6).reshape(heads, width, 3 * HEAD)

    scalars = jnp.stack(
        [live_count, lax.axis_index("g"), lax.axis_index("c"), lax.axis_index("a")]
    )
    out, query, key, value = attention_forward(scene_tokens, pieces, group_weight, n_g)
    back = [out[0]] + [shift(out[k], "g", k) for k in range(1, n_g)]
    made = middle(scalars, tokens, cotangent, gain_two[None], back, weights, n_a)
    mixed, grad_resid, sends = made[0], made[1], made[2 : 2 + 2 * n_g]
    made = made[2 + 2 * n_g :]
    grad_blocks = [made[: n_a * n_c], made[n_a * n_c :]]

    come = [[shift(block, "c", 1) for block in some[n_a:]] for some in grad_blocks]

    columns = heads * 3 * HEAD
    padded = -(-columns // LANES) * LANES
    turned = qkv_low.reshape(share, 3, n_g, heads, HEAD).transpose(0, 2, 3, 1, 4)
    turned = turned.reshape(share, n_g, columns)
    qkv_weight = jnp.pad(turned, ((0, 0), (0, 0), (0, padded - columns)))
    qkv_weight = after(qkv_weight.reshape(share, n_g * padded), *ready)
    qkv_weight = lax.all_gather(qkv_weight, ALL, axis=0, tiled=True)

    grads = [[sends[0]] + [shift(sends[k], "g", -k) for k in range(1, n_g)]]
    some = [after(block, *grads[0]) for block in sends[n_g:]]
    grads += [[some[0]] + [shift(some[k], "g", -k) for k in range(1, n_g)]] * (heads - 1)

    made = []
    grad_pieces = []
    whole = []

    def finish(head):
        own, across, grad_query = made[head]
        own = after(own, made[min(head + 1, heads - 1)][0])
        if head >= 2:
            own = after(own, *whole[head - 2])
        done = combine(own, grad_query, across)
        grad_pieces.append(done)
        whole.append([done[0]] + [shift(done[k], "g", k) for k in range(1, n_g)])

    for head in range(heads):
        gate = []
        if head == 1:
            come = [[after(block, made[0][0], *grads[1]) for block in some] for some in come]
            far = [
                [add_low(*pair) for pair in zip(some[1:n_a], there[1:])]
                for some, there in zip(grad_blocks, come)
            ]
            gate = far[0] + far[1]
            far[0] = [shift(block, "a", k) for k, block in enumerate(far[0], 1)]
        if head >= 2:
            finish(head - 2)
            gate = [*grad_pieces[head - 2], qkv_weight]
        gated = grads[head]
        if gate:
            gated = [after(gated[0], *gate)] + gated[1:]
        own, across, grad_query = attention_backward(out, query, key, value, gated, head)
        across = [
            shift(across[(j - 1) * n_g : j * n_g] if n_r > 2 else across, "r", j)
            for j in range(1, n_r)
        ]
        made.append((own, across, grad_query))
    made[-2] = (after(made[-2][0], *whole[-1]),) + made[-2][1:]
    finish(heads - 2)
    far[0] = [after(block, *grad_pieces[-1]) for block in far[0]]
    first = add_high(grad_blocks[0][0], come[0][0], *far[0])
    first, send = halves(first.reshape(n_g, n_r, share, -1), "r", 1)
    far[1] = [after(block, *far[0]) for block in far[1]]
    made[-1] = (after(made[-1][0], *send),) + made[-1][1:]
    finish(heads - 1)
    send = [shift(after(block, *made[-1][1]), "r", j) for j, block in enumerate(send, 1)]
    far[1] = [shift(block, "a", k) for k, block in enumerate(far[1], 1)]
    second = add_high(grad_blocks[1][0], come[1][0], *far[1]).reshape(n_g, n_r, share, -1)
    second = scatter_sum(second, "r", 1).astype(BF16)
    grad_pieces = [[some[k] for some in grad_pieces] for k in range(n_g)]
    whole = [[some[k] for some in whole] for k in range(n_g)]

    grad_pieces[0][0] = after(grad_pieces[0][0], *(some[-2] for some in whole))
    mine, theirs = group_grad(scalars, own_pieces, grad_pieces, n_a, n_c)
    theirs = after(theirs, *(some[-1] for some in whole), *send)
    first = lax.all_to_all(add_low(first, *send), "g", 0, 0)
    qkv_grad = add_high(mine, shift(theirs, "c", 1))
    qkv_grad = qkv_grad.reshape(n_a, n_g, n_r, share, columns)
    qkv_grad = scatter_sum(after(scatter_sum(qkv_grad, "a", 0), first), "r", 1)
    second = jnp.concatenate([second, qkv_grad.astype(BF16)], axis=2)
    second = lax.all_to_all(after(second, first), "g", 0, 0)
    input_grad = input_gradient(scalars, tokens, grad_resid, gain_one[None], qkv_weight, whole)

    first = jnp.sum(first.astype(F32), axis=0)
    out_share = first[:, :width]
    up_share = first[:, width:]
    second_share = jnp.sum(up_turned.astype(F32) * up_share, axis=1)
    up_share = (
        up_share.reshape(share, wide, n_all, share).transpose(0, 2, 1, 3).reshape(share, hidden)
    )
    place = lax.axis_index(ALL) * share
    own_gain_one = lax.dynamic_slice_in_dim(gain_one, place, share)
    own_gain_two = lax.dynamic_slice_in_dim(gain_two, place, share)
    second_share = second_share / own_gain_two
    down_share, qkv_share, first_share = last_shares(
        second, turned.swapaxes(0, 1), own_gain_one[:, None]
    )
    down_share = down_share.reshape(wide * share, width)
    first_share = first_share[:, 0]
    return (
        mixed,
        input_grad,
        qkv_share,
        out_share,
        up_share,
        down_share,
        first_share,
        second_share,
    )


def solution(mesh):
    n_scene, n_seq = mesh.devices.shape
    n_g = math.gcd(HEADS, n_seq)
    inner = Mesh(mesh.devices.reshape(n_scene // 2, 2, n_g, n_seq // n_g), ALL)
    split = P(ALL, None)
    in_specs = (split, P(("a", "c")), split, split, split, split, split, P(), P())
    out_specs = (split, split, split, split, split, split, P(ALL), P(ALL))
    return jax.shard_map(
        on_device, mesh=inner, in_specs=in_specs, out_specs=out_specs, check_vma=False
    )
```

```python
import functools
import math

import jax
import jax.numpy as jnp
from jax import lax
from jax.experimental import pallas as pl
from jax.experimental.pallas import tpu as pltpu
from jax.sharding import Mesh
from jax.sharding import PartitionSpec as P

HEADS = 12
HEAD = 64
LANES = 128
NEG_BIG = -1e30
EPS = 1e-05
SCALE = 0.125
EXP_SCALE = SCALE * math.log2(math.e)
VMEM_LIMIT = 60 * 1024 * 1024
GELU_A = math.sqrt(2.0 / math.pi)
GELU_B = 0.044715
F32 = jnp.float32
BF16 = jnp.bfloat16
ALL = ("a", "c", "g", "r")


def nt(left, right):
    return lax.dot_general(left, right, (((1,), (1,)), ((), ())), preferred_element_type=F32)


def nn(left, right):
    return lax.dot_general(left, right, (((1,), (0,)), ((), ())), preferred_element_type=F32)


def tn(left, right):
    return lax.dot_general(left, right, (((0,), (0,)), ((), ())), preferred_element_type=F32)


def three_parts(value):
    first = value.astype(BF16)
    rest = value - first.astype(F32)
    second = rest.astype(BF16)
    third = (rest - second.astype(F32)).astype(BF16)
    return first, second, third


def block_rows(rows):
    return 256 if rows % 256 == 0 else rows


def attention_forward_kernel(n_own, live_ref, *refs):
    n_pieces = len(refs) - 6
    pieces, weight = refs[:n_pieces], refs[n_pieces]
    out_ref, query_ref, key_ref, value_ref, out_scr = refs[n_pieces + 1 :]
    rows = pieces[0].shape[0]
    half = rows // 2
    lane = lax.broadcasted_iota(jnp.int32, (rows, HEAD), 1)
    slot = lax.broadcasted_iota(jnp.int32, (rows, HEAD), 0)
    bias = jnp.where(slot < live_ref[0], 0.0, NEG_BIG)
    key_extra = jnp.where(lane == 0, bias, jnp.where(lane < 4, 1.0, 0.0)).astype(BF16)
    value_extra = jnp.where(lane < 3, 1.0, 0.0).astype(BF16)
    query_extra = jnp.where(lane == 0, 1.0, 0.0).astype(BF16)
    for index in range(n_pieces):
        made = nn(pieces[index][...], weight[0]).astype(BF16)
        here = slice(index * rows, (index + 1) * rows)
        key_ref[0, here, :] = jnp.concatenate([made[:, HEAD : 2 * HEAD], key_extra], axis=1)
        value_ref[0, here, :] = jnp.concatenate([made[:, 2 * HEAD :], value_extra], axis=1)
        if index < n_own:
            query_ref[0, here, :] = jnp.concatenate([made[:, :HEAD], query_extra], axis=1)

    size = block_rows(rows * n_own)
    blocks = rows * n_own // size
    full = lax.broadcasted_iota(jnp.int32, (size, LANES), 1)
    keys = key_ref[0]
    values = value_ref[0]
    scores = nt(query_ref[0, :size], keys)
    for block in range(blocks):
        here = slice(block * size, (block + 1) * size)
        later = None
        if block + 1 < blocks:
            later = nt(query_ref[0, (block + 1) * size : (block + 2) * size], keys)
        highest = jnp.max(scores, axis=1, keepdims=True)
        weights = jnp.exp2((scores - highest) * EXP_SCALE).astype(BF16)
        summed = nn(weights, values)
        total = summed[:, HEAD : HEAD + 1]
        out_scr[here, :] = summed / total
        first, second, third = three_parts(-(highest + jnp.log2(total) * (1.0 / EXP_SCALE)))
        query_ref[0, here, :] = jnp.where(
            full == HEAD + 1,
            first,
            jnp.where(
                full == HEAD + 2, second, jnp.where(full == HEAD + 3, third, query_ref[0, here, :])
            ),
        )
        scores = later
    for index in range(n_own):
        base = index * rows
        upper = out_scr[base : base + half, :HEAD]
        lower = out_scr[base + half : base + rows, :HEAD]
        out_ref[index, 0] = jnp.concatenate([upper, lower], axis=1).astype(BF16)


def attention_forward(live, pieces, weight, n_own):
    heads = weight.shape[0]
    rows, width = pieces[0].shape
    n_keys = rows * len(pieces)
    n_queries = rows * n_own
    half = rows // 2
    per_head = lambda n: pl.BlockSpec((1, n, LANES), lambda h: (h, 0, 0))
    return pl.pallas_call(
        functools.partial(attention_forward_kernel, n_own),
        grid=(heads,),
        in_specs=[pl.BlockSpec(memory_space=pltpu.SMEM)]
        + [pl.BlockSpec((rows, width), lambda h: (0, 0), pipeline_mode=pl.Buffered(1)) for _ in pieces]
        + [pl.BlockSpec((1, width, 3 * HEAD), lambda h: (h, 0, 0))],
        out_specs=[
            pl.BlockSpec((n_own, 1, half, LANES), lambda h: (0, h, 0, 0)),
            per_head(n_queries),
            per_head(n_keys),
            per_head(n_keys),
        ],
        out_shape=[
            jax.ShapeDtypeStruct((n_own, heads, half, LANES), BF16),
            jax.ShapeDtypeStruct((heads, n_queries, LANES), BF16),
            jax.ShapeDtypeStruct((heads, n_keys, LANES), BF16),
            jax.ShapeDtypeStruct((heads, n_keys, LANES), BF16),
        ],
        scratch_shapes=[pltpu.VMEM((n_queries, LANES), F32)],
        compiler_params=pltpu.CompilerParams(
            dimension_semantics=("arbitrary",), vmem_limit_bytes=VMEM_LIMIT
        ),
        name="attention_forward",
    )(live, *pieces, weight)


def attention_backward_kernel(rows, n_own, out_ref, query_ref, key_ref, value_ref, *refs):
    grads = refs[:n_own]
    own_ref, send_ref, grad_query_ref, grad_scr, low_scr, key_scr, query_scr, acc_scr = refs[n_own:]
    half = rows // 2
    lane = lax.broadcasted_iota(jnp.int32, (rows, HEAD), 1)
    for index in range(n_own):
        packed = grads[index][...]
        grad = jnp.concatenate([packed[:, :HEAD], packed[:, HEAD:]], axis=0)
        packed_out = out_ref[index, 0]
        attended = jnp.concatenate([packed_out[:, :HEAD], packed_out[:, HEAD:]], axis=0)
        delta = jnp.sum(grad.astype(F32) * attended.astype(F32), axis=1, keepdims=True)
        first, second, third = three_parts(-delta)
        zeros = jnp.zeros_like(grad)
        extra = jnp.where(
            lane == 0, first, jnp.where(lane == 1, second, jnp.where(lane == 2, third, zeros))
        )
        here = slice(index * rows, (index + 1) * rows)
        grad_scr[here, :] = jnp.concatenate([grad, extra], axis=1)
        low_scr[here, :] = jnp.concatenate([zeros, grad], axis=1)
    key_scr[...] = key_ref[0].T

    size = block_rows(rows * n_own)
    blocks = rows * n_own // size
    keys = key_ref[0]
    values = value_ref[0]
    full = lax.broadcasted_iota(jnp.int32, (size, LANES), 1)

    def products(block):
        here = slice(block * size, (block + 1) * size)
        return nt(keys, query_ref[0, here, :]), nt(values, grad_scr[here, :])

    scores, change = products(0)
    for block in range(blocks):
        here = slice(block * size, (block + 1) * size)
        later = products(block + 1) if block + 1 < blocks else (None, None)
        weights = jnp.exp2(scores * EXP_SCALE)
        dscore = (weights * change).astype(BF16)
        query = query_ref[0, here, :]
        plain = jnp.where(full < HEAD, query * SCALE, jnp.zeros_like(query))
        terms = nn(
            jnp.concatenate([weights.astype(BF16), dscore], axis=1),
            jnp.concatenate([low_scr[here, :], plain], axis=0),
        )
        if block == 0:
            acc_scr[...] = terms
        else:
            acc_scr[...] += terms
        query_scr[here, :] = nn(key_scr[...], dscore).T * SCALE
        scores, change = later
    for index in range(n_own):
        base = index * rows
        upper = query_scr[base : base + half, :HEAD]
        lower = query_scr[base + half : base + rows, :HEAD]
        grad_query_ref[index] = jnp.concatenate([upper, lower], axis=1).astype(BF16)
        own_ref[index] = acc_scr[base : base + rows, :]
    for index in range(send_ref.shape[0]):
        base = (n_own + index) * rows
        send_ref[index] = acc_scr[base : base + rows, :].astype(BF16)


def attention_backward(out, query, key, value, grads, head):
    n_own, _, half, _ = out.shape
    rows = 2 * half
    n_queries, n_keys = query.shape[1], key.shape[1]
    n_send = n_keys // rows - n_own
    per_head = lambda n: pl.BlockSpec((1, n, LANES), lambda i: (head, 0, 0))
    stacked = lambda k, n: pl.BlockSpec((k, 1, n, LANES), lambda i: (0, head, 0, 0))
    vmem = pl.BlockSpec(memory_space=pltpu.VMEM)
    return pl.pallas_call(
        functools.partial(attention_backward_kernel, rows, n_own),
        grid=(1,),
        in_specs=[stacked(n_own, half), per_head(n_queries), per_head(n_keys), per_head(n_keys)]
        + [
            pl.BlockSpec((None, half, LANES), lambda i: (head - 1, 0, 0)) if head else vmem
            for _ in grads
        ],
        out_specs=[vmem, vmem, vmem],
        out_shape=[
            jax.ShapeDtypeStruct((n_own, rows, LANES), F32),
            jax.ShapeDtypeStruct((n_send, rows, LANES), BF16),
            jax.ShapeDtypeStruct((n_own, half, LANES), BF16),
        ],
        scratch_shapes=[
            pltpu.VMEM((n_queries, LANES), BF16),
            pltpu.VMEM((n_queries, LANES), BF16),
            pltpu.VMEM((LANES, n_keys), BF16),
            pltpu.VMEM((n_queries, LANES), F32),
            pltpu.VMEM((n_keys, LANES), F32),
        ],
        compiler_params=pltpu.CompilerParams(
            dimension_semantics=("arbitrary",), vmem_limit_bytes=VMEM_LIMIT
        ),
        name="attention_backward",
    )(out, query, key, value, *grads)


def unpack_rows(packed):
    heads = packed.shape[0]
    return jnp.concatenate(
        [
            jnp.concatenate([packed[h, :, :HEAD], packed[h, :, HEAD:]], axis=0)
            for h in range(heads)
        ],
        axis=1,
    )


def middle_kernel(sizes, scalar_ref, *refs):
    n_g, wide, width, rows, n_a, chunks = sizes
    refs = list(refs)
    part = width // n_g
    heads = part // HEAD

    def take(count):
        taken = refs[:count]
        del refs[:count]
        return taken

    token_ref, cotangent_ref, gain_ref = take(3)
    pieces = take(n_g)
    (weight_hbm,) = take(1)
    mixed_ref, resid_ref = take(2)
    grads = take(2 * n_g)
    grad_hbm = [take(2 * n_a) for _ in chunks]
    weight_scr, made_scr, attended_scr, in_sem, out_sem = refs
    half = rows // 2
    block = width // (2 * n_a)
    here_a, here_c = scalar_ref[3], scalar_ref[2]

    def row_block(step_a, step_c):
        at_a = here_a + step_a
        at_a = jnp.where(at_a >= n_a, at_a - n_a, at_a)
        at_c = jnp.where(here_c + step_c >= 2, 0, here_c + step_c)
        return pl.ds(pl.multiple_of((at_a * 2 + at_c) * block, block), block)

    def chunk_of(index):
        first = 0
        for number, count in enumerate(chunks):
            if index < first + count:
                return number, pl.ds((index - first) * width, width)
            first += count

    def fetch(index):
        return [
            pltpu.make_async_copy(
                weight_hbm.at[:, pl.ds(index * width, width)],
                weight_scr.at[index],
                in_sem.at[index],
            )
        ]

    def flush(index):
        number, columns = chunk_of(index)
        return [
            pltpu.make_async_copy(
                made_scr.at[index, row_block(step_a, step_c)],
                grad_hbm[number][step_c * n_a + step_a].at[:, columns],
                out_sem.at[index, step_c * n_a + step_a],
            )
            for step_c in range(2)
            for step_a in range(n_a)
        ]

    def start(copies):
        for copy in copies:
            copy.start()

    def wait(copies):
        for copy in copies:
            copy.wait()

    count = 1 + 2 * wide
    for index in [0] + [at + q for q in range(wide) for at in (1, 1 + wide)]:
        start(fetch(index))

    def places(k):
        at = scalar_ref[1] - k
        at = jnp.where(at < 0, at + n_g, at)
        return pl.ds(pl.multiple_of(at * part, part), part)

    resid = token_ref[...].astype(F32)
    for k in range(n_g):
        attended_scr[k] = unpack_rows(pieces[k][...])
    wait(fetch(0))
    for k in range(n_g):
        resid = resid + nn(attended_scr[k], weight_scr[0, places(k), :])
    gain = gain_ref[...]
    mean = jnp.mean(resid, axis=1, keepdims=True)
    centered = resid - mean
    inverse = lax.rsqrt(jnp.mean(centered * centered, axis=1, keepdims=True) + EPS)
    scaled = centered * inverse
    normed = (scaled * gain).astype(BF16)
    slot = lax.broadcasted_iota(jnp.int32, (rows, width), 0)
    grad_low = jnp.where(
        slot < scalar_ref[0], cotangent_ref[...].astype(F32), 0.0
    ).astype(BF16)
    normed_turned = normed.T
    added = None
    grad_normed = None
    for q in range(wide):
        up_at, down_at = 1 + q, 1 + wide + q
        wait(fetch(up_at))
        upper = nn(normed, weight_scr[up_at])
        wait(fetch(down_at))
        grad_active = nt(grad_low, weight_scr[down_at])
        square = upper * upper
        inner = jnp.tanh((GELU_A * upper) * (1.0 + GELU_B * square))
        onward = 0.5 * (1.0 + inner)
        active = (upper * onward).astype(BF16)
        slope = onward + (0.5 * GELU_A) * upper * (1.0 - inner * inner) * (
            1.0 + (3.0 * GELU_B) * square
        )
        grad_upper = (grad_active * slope).astype(BF16)
        more = nn(active, weight_scr[down_at])
        added = more if added is None else added + more
        made_scr[down_at] = tn(active, grad_low).astype(BF16)
        start(flush(down_at))
        made_scr[up_at] = nn(normed_turned, grad_upper).astype(BF16)
        start(flush(up_at))
        more = nt(grad_upper, weight_scr[up_at])
        grad_normed = more if grad_normed is None else grad_normed + more
    mixed_ref[...] = (resid + added).astype(BF16)
    grad_scaled = grad_normed * gain
    first = jnp.mean(grad_scaled, axis=1, keepdims=True)
    second = jnp.mean(grad_scaled * scaled, axis=1, keepdims=True)
    grad_resid = grad_low.astype(F32) + inverse * (grad_scaled - first - scaled * second)
    resid_ref[...] = grad_resid
    branch = grad_resid.astype(BF16)
    for k in range(n_g):
        grad_block = nt(branch, weight_scr[0, places(k), :])
        for h in range(heads):
            here = slice(h * HEAD, (h + 1) * HEAD)
            packed = jnp.concatenate([grad_block[:half, here], grad_block[half:, here]], axis=1)
            if h == 0:
                grads[k][...] = packed.astype(BF16)
            else:
                grads[n_g + k][h - 1] = packed.astype(BF16)
    for k in range(n_g):
        made_scr[0, places(k), :] = tn(attended_scr[k], branch).astype(BF16)
    start(flush(0))
    for index in range(count):
        wait(flush(index))


def middle(scalars, tokens, cotangent, gain, pieces, weights, n_a):
    rows, width = tokens.shape
    n_g = len(pieces)
    heads, half, _ = pieces[0].shape
    count = weights.shape[1] // width
    wide = (count - 1) // 2
    chunks = (1 + 2 * (wide // 2), 2 * (wide - wide // 2))
    vmem = pl.BlockSpec(memory_space=pltpu.VMEM)
    anywhere = pl.BlockSpec(memory_space=pl.ANY)
    flat = [
        jax.ShapeDtypeStruct((width // (2 * n_a), chunk * width), BF16)
        for chunk in chunks
        for _ in range(2 * n_a)
    ]
    return pl.pallas_call(
        functools.partial(middle_kernel, (n_g, wide, width, rows, n_a, chunks)),
        in_specs=[pl.BlockSpec(memory_space=pltpu.SMEM)] + [vmem] * (3 + n_g) + [anywhere],
        out_specs=[vmem] * (2 + 2 * n_g) + [anywhere] * len(flat),
        out_shape=[
            jax.ShapeDtypeStruct((rows, width), BF16),
            jax.ShapeDtypeStruct((rows, width), F32),
        ]
        + [jax.ShapeDtypeStruct((half, LANES), BF16)] * n_g
        + [jax.ShapeDtypeStruct((heads - 1, half, LANES), BF16)] * n_g
        + flat,
        scratch_shapes=[
            pltpu.VMEM((count, width, width), BF16),
            pltpu.VMEM((count, width, width), BF16),
            pltpu.VMEM((n_g, rows, width // n_g), BF16),
            pltpu.SemaphoreType.DMA((count,)),
            pltpu.SemaphoreType.DMA((count, 2 * n_a)),
        ],
        compiler_params=pltpu.CompilerParams(vmem_limit_bytes=VMEM_LIMIT),
        name="middle",
    )(scalars, tokens, cotangent, gain, *pieces, weights)


def combine_kernel(rows, n_terms, own_ref, query_ref, *refs):
    terms, outs = refs[:n_terms], refs[n_terms:]
    for k, out_ref in enumerate(outs):
        total = own_ref[k]
        for term in terms:
            total = total + term[k].astype(F32)
        out_ref[:rows, :] = total.astype(BF16)
        out_ref[rows:, :] = query_ref[k]


def combine(own, grad_query, terms):
    n_g, rows, _ = own.shape
    vmem = pl.BlockSpec(memory_space=pltpu.VMEM)
    shape = (rows + grad_query.shape[1], LANES)
    return pl.pallas_call(
        functools.partial(combine_kernel, rows, len(terms)),
        in_specs=[vmem] * (2 + len(terms)),
        out_specs=[vmem] * n_g,
        out_shape=[jax.ShapeDtypeStruct(shape, BF16)] * n_g,
        compiler_params=pltpu.CompilerParams(vmem_limit_bytes=VMEM_LIMIT),
        name="combine",
    )(own, grad_query, *terms)


def unpack_grads(pieces, rows):
    parts = []
    for piece in pieces:
        packed = piece[rows:, :]
        parts.append(jnp.concatenate([packed[:, :HEAD], packed[:, HEAD:]], axis=0))
        parts.append(piece[:rows, :])
    return jnp.concatenate(parts, axis=1)


def group_grad_kernel(n_g, n_a, scalar_ref, *refs):
    inputs, pieces = refs[:n_g], refs[n_g:-3]
    mine_ref, other_ref, scr = refs[-3:]
    heads = len(pieces) // n_g
    rows = inputs[0].shape[0]
    left = jnp.concatenate([ref[...] for ref in inputs], axis=0)
    right = [
        unpack_grads([ref[...] for ref in pieces[k * heads : (k + 1) * heads]], rows)
        for k in range(n_g)
    ]
    right = jnp.concatenate(right, axis=0)
    scr[...] = tn(left, right)
    block = mine_ref.shape[1]
    n_c = scr.shape[0] // (n_a * block)
    for a in range(n_a):
        mine = pl.ds(pl.multiple_of((a * n_c + scalar_ref[2]) * block, block), block)
        other = pl.ds(pl.multiple_of((a * n_c + n_c - 1 - scalar_ref[2]) * block, block), block)
        mine_ref[a] = scr[mine, :]
        other_ref[a] = scr[other, :].astype(BF16)


def group_grad(scalars, inputs, pieces, n_a, n_c):
    rows, width = inputs[0].shape
    n_g = len(pieces)
    heads = len(pieces[0])
    columns = heads * 3 * HEAD
    block = width // (n_a * n_c)
    vmem = pl.BlockSpec(memory_space=pltpu.VMEM)
    return pl.pallas_call(
        functools.partial(group_grad_kernel, n_g, n_a),
        in_specs=[pl.BlockSpec(memory_space=pltpu.SMEM)] + [vmem] * (n_g * (1 + heads)),
        out_specs=[vmem] * 2,
        out_shape=[
            jax.ShapeDtypeStruct((n_a, block, columns), F32),
            jax.ShapeDtypeStruct((n_a, block, columns), BF16),
        ],
        scratch_shapes=[pltpu.VMEM((width, columns), F32)],
        compiler_params=pltpu.CompilerParams(vmem_limit_bytes=VMEM_LIMIT),
        name="group_grad",
    )(scalars, *inputs, *(piece for some in pieces for piece in some))


def input_grad_kernel(n_g, scalar_ref, token_ref, resid_ref, gain_ref, weight_ref, *refs):
    pieces, (out_ref, scr) = refs[:-2], refs[-2:]
    heads = len(pieces) // n_g
    rows, width = token_ref.shape
    padded = scr.shape[2]
    for k in range(n_g):
        at = scalar_ref[1] - k
        at = jnp.where(at < 0, at + n_g, at)
        made = unpack_grads([ref[...] for ref in pieces[k * heads : (k + 1) * heads]], rows)
        pad = jnp.zeros((rows, padded - made.shape[1]), BF16)
        scr[at] = jnp.concatenate([made, pad], axis=1)
    grad = nt(scr[0], weight_ref[:, :padded])
    for k in range(1, n_g):
        grad = grad + nt(scr[k], weight_ref[:, k * padded : (k + 1) * padded])
    values = token_ref[...].astype(F32)
    mean = jnp.mean(values, axis=1, keepdims=True)
    centered = values - mean
    inverse = lax.rsqrt(jnp.mean(centered * centered, axis=1, keepdims=True) + EPS)
    scaled = centered * inverse
    grad_scaled = grad * gain_ref[...]
    first = jnp.mean(grad_scaled, axis=1, keepdims=True)
    second = jnp.mean(grad_scaled * scaled, axis=1, keepdims=True)
    out_ref[...] = resid_ref[...] + inverse * (grad_scaled - first - scaled * second)


def input_gradient(scalars, tokens, grad_resid, gain, weight, pieces):
    rows, width = tokens.shape
    n_g = len(pieces)
    flat = [piece for some in pieces for piece in some]
    vmem = pl.BlockSpec(memory_space=pltpu.VMEM)
    return pl.pallas_call(
        functools.partial(input_grad_kernel, n_g),
        in_specs=[pl.BlockSpec(memory_space=pltpu.SMEM)] + [vmem] * (4 + len(flat)),
        out_specs=vmem,
        out_shape=jax.ShapeDtypeStruct((rows, width), F32),
        scratch_shapes=[pltpu.VMEM((n_g, rows, weight.shape[1] // n_g), BF16)],
        compiler_params=pltpu.CompilerParams(vmem_limit_bytes=VMEM_LIMIT),
        name="input_gradient",
    )(scalars, tokens, grad_resid, gain, weight, *flat)


def share_kernel(wide, got_ref, weight_ref, gain_ref, down_ref, qkv_ref, norm_ref):
    n_g, share, columns = weight_ref.shape
    heads = columns // (3 * HEAD)
    width = n_g * heads * HEAD
    for q in range(wide):
        here = slice(q * width, (q + 1) * width)
        total = got_ref[0, :, here].astype(F32)
        for g in range(1, n_g):
            total = total + got_ref[g, :, here].astype(F32)
        down_ref[q] = total
    norm = jnp.zeros((share, 1), F32)
    for g in range(n_g):
        made = got_ref[g, :, wide * width :].astype(F32)
        norm = norm + jnp.sum(made * weight_ref[g].astype(F32), axis=1, keepdims=True)
        for h in range(heads):
            for part in range(3):
                start = part * width + (g * heads + h) * HEAD
                at = (h * 3 + part) * HEAD
                qkv_ref[:, start : start + HEAD] = made[:, at : at + HEAD]
    row = lax.broadcasted_iota(jnp.int32, (share, share), 0)
    column = lax.broadcasted_iota(jnp.int32, (share, share), 1)
    norm_ref[...] = jnp.sum(
        jnp.where(row == column, norm / gain_ref[...], 0.0), axis=0, keepdims=True
    )


def last_shares(got, weight, gain):
    n_g, share, columns = weight.shape
    width = n_g * columns // 3
    wide = (got.shape[2] - columns) // width
    vmem = pl.BlockSpec(memory_space=pltpu.VMEM)
    return pl.pallas_call(
        functools.partial(share_kernel, wide),
        in_specs=[vmem] * 3,
        out_specs=[vmem] * 3,
        out_shape=[
            jax.ShapeDtypeStruct((wide, share, width), F32),
            jax.ShapeDtypeStruct((share, 3 * width), F32),
            jax.ShapeDtypeStruct((1, share), F32),
        ],
        compiler_params=pltpu.CompilerParams(vmem_limit_bytes=VMEM_LIMIT),
        name="last_shares",
    )(got, weight, gain)


def norm_rows(values, gain_vector):
    mean_value = jnp.mean(values, axis=-1, keepdims=True)
    centered = values - mean_value
    variance = jnp.mean(centered * centered, axis=-1, keepdims=True)
    return centered * lax.rsqrt(variance + EPS) * gain_vector


def shift(value, axis, step):
    n = lax.axis_size(axis)
    return lax.ppermute(value, axis, [(i, (i + step) % n) for i in range(n)])


def gather(value, axis):
    n = lax.axis_size(axis)
    if n == 1:
        return value[None]
    if n == 2:
        other = shift(value, axis, 1)
        first = lax.axis_index(axis) == 0
        return jnp.stack([jnp.where(first, value, other), jnp.where(first, other, value)])
    return lax.all_gather(value, axis, axis=0)


def after(value, *others):
    return lax.optimization_barrier((value,) + others)[0]


def add_high(*terms):
    total = terms[0].astype(F32)
    for term in terms[1:]:
        total = total + term.astype(F32)
    return total


def add_low(*terms):
    return add_high(*terms).astype(BF16)


def halves(value, axis, dim):
    n = lax.axis_size(axis)
    me = lax.axis_index(axis)
    mine = lax.dynamic_index_in_dim(value, me, dim, keepdims=False)
    others = [
        lax.dynamic_index_in_dim(value, (me + j) % n, dim, keepdims=False).astype(BF16)
        for j in range(1, n)
    ]
    return mine, others


def sum_halves(mine, others, axis):
    return add_high(mine, *(shift(other, axis, j) for j, other in enumerate(others, 1)))


def scatter_sum(value, axis, dim):
    return sum_halves(*halves(value, axis, dim), axis)


def on_device(
    tokens,
    scene_tokens,
    cotangent,
    qkv_master,
    out_master,
    up_master,
    down_master,
    gain_one,
    gain_two,
):
    rows, width = tokens.shape
    hidden = up_master.shape[1]
    n_a, n_c, n_g, n_r = (lax.axis_size(axis) for axis in ALL)
    share = qkv_master.shape[0]
    wide = hidden // width
    heads = HEADS // n_g
    live_count = scene_tokens[0]

    normed_low = norm_rows(tokens.astype(F32), gain_one).astype(BF16)
    qkv_low = qkv_master.astype(BF16)
    parts = qkv_low.reshape(share, 3, n_g, heads, HEAD).transpose(2, 0, 3, 1, 4)
    parts = parts.reshape(n_g, share, heads * 3 * HEAD)
    own_pieces = [normed_low] * n_g
    for k in {1, n_g - 1}:
        own_pieces[k] = shift(normed_low, "g", -k)
    ready = [own_pieces[1], own_pieces[n_g - 1]]
    others = {(j, 0): shift(normed_low, "r", -j) for j in range(1, n_r)}
    ready += others.values()
    parts = lax.all_to_all(parts, "g", 0, 0)
    ready.append(parts)
    for k in range(2, n_g - 1):
        own_pieces[k] = shift(after(own_pieces[k - 1], *ready), "g", -1)
    for k in sorted(range(1, n_g), key=lambda k: min(k, n_g - k)):
        for j in range(1, n_r):
            others[j, k] = shift(after(own_pieces[k], *ready), "r", -j)
    pieces = own_pieces + [others[at] for at in sorted(others)]

    n_all = n_a * n_c * n_g * n_r
    up_turned = (
        up_master.astype(BF16)
        .reshape(share, n_all, wide, share)
        .transpose(0, 2, 1, 3)
        .reshape(share, hidden)
    )
    down_turned = down_master.astype(BF16).reshape(wide, share, width)
    packed = jnp.concatenate([out_master.astype(BF16), up_turned, *down_turned], axis=1)
    weights = lax.all_gather(packed, ALL, axis=0, tiled=True)

    parts = gather(gather(gather(after(parts, *ready), "r"), "c"), "a")
    parts = parts.reshape(n_a, n_c, n_r, n_g, share, heads, 3 * HEAD)
    group_weight = parts.transpose(5, 0, 1, 3, 2, 4, 6).reshape(heads, width, 3 * HEAD)

    scalars = jnp.stack(
        [live_count, lax.axis_index("g"), lax.axis_index("c"), lax.axis_index("a")]
    )
    out, query, key, value = attention_forward(scene_tokens, pieces, group_weight, n_g)
    back = [out[0]] + [shift(out[k], "g", k) for k in range(1, n_g)]
    made = middle(scalars, tokens, cotangent, gain_two[None], back, weights, n_a)
    mixed, grad_resid, sends = made[0], made[1], made[2 : 2 + 2 * n_g]
    made = made[2 + 2 * n_g :]
    grad_blocks = [made[: n_a * n_c], made[n_a * n_c :]]

    come = [[shift(block, "c", 1) for block in some[n_a:]] for some in grad_blocks]

    columns = heads * 3 * HEAD
    padded = -(-columns // LANES) * LANES
    turned = qkv_low.reshape(share, 3, n_g, heads, HEAD).transpose(0, 2, 3, 1, 4)
    turned = turned.reshape(share, n_g, columns)
    qkv_weight = jnp.pad(turned, ((0, 0), (0, 0), (0, padded - columns)))
    qkv_weight = after(qkv_weight.reshape(share, n_g * padded), *ready)
    qkv_weight = lax.all_gather(qkv_weight, ALL, axis=0, tiled=True)

    grads = [[sends[0]] + [shift(sends[k], "g", -k) for k in range(1, n_g)]]
    some = [after(block, *grads[0]) for block in sends[n_g:]]
    grads += [[some[0]] + [shift(some[k], "g", -k) for k in range(1, n_g)]] * (heads - 1)

    made = []
    grad_pieces = []
    whole = []

    def finish(head):
        own, across, grad_query = made[head]
        own = after(own, made[min(head + 1, heads - 1)][0])
        if head >= 2:
            own = after(own, *whole[head - 2])
        done = combine(own, grad_query, across)
        grad_pieces.append(done)
        whole.append([done[0]] + [shift(done[k], "g", k) for k in range(1, n_g)])

    for head in range(heads):
        gate = []
        if head == 1:
            come = [[after(block, made[0][0], *grads[1]) for block in some] for some in come]
            far = [
                [add_low(*pair) for pair in zip(some[1:n_a], there[1:])]
                for some, there in zip(grad_blocks, come)
            ]
            gate = far[0] + far[1]
            far[0] = [shift(block, "a", k) for k, block in enumerate(far[0], 1)]
        if head >= 2:
            finish(head - 2)
            gate = [*grad_pieces[head - 2], qkv_weight]
        gated = grads[head]
        if gate:
            gated = [after(gated[0], *gate)] + gated[1:]
        own, across, grad_query = attention_backward(out, query, key, value, gated, head)
        across = [
            shift(across[(j - 1) * n_g : j * n_g] if n_r > 2 else across, "r", j)
            for j in range(1, n_r)
        ]
        made.append((own, across, grad_query))
    made[-2] = (after(made[-2][0], *whole[-1]),) + made[-2][1:]
    finish(heads - 2)
    far[0] = [after(block, *grad_pieces[-1]) for block in far[0]]
    first = add_high(grad_blocks[0][0], come[0][0], *far[0])
    first, send = halves(first.reshape(n_g, n_r, share, -1), "r", 1)
    far[1] = [after(block, *far[0]) for block in far[1]]
    made[-1] = (after(made[-1][0], *send),) + made[-1][1:]
    finish(heads - 1)
    send = [shift(after(block, *made[-1][1]), "r", j) for j, block in enumerate(send, 1)]
    far[1] = [shift(block, "a", k) for k, block in enumerate(far[1], 1)]
    second = add_high(grad_blocks[1][0], come[1][0], *far[1]).reshape(n_g, n_r, share, -1)
    second = scatter_sum(second, "r", 1).astype(BF16)
    grad_pieces = [[some[k] for some in grad_pieces] for k in range(n_g)]
    whole = [[some[k] for some in whole] for k in range(n_g)]

    grad_pieces[0][0] = after(grad_pieces[0][0], *(some[-2] for some in whole))
    mine, theirs = group_grad(scalars, own_pieces, grad_pieces, n_a, n_c)
    theirs = after(theirs, *(some[-1] for some in whole), *send)
    first = lax.all_to_all(add_low(first, *send), "g", 0, 0)
    qkv_grad = add_high(mine, shift(theirs, "c", 1))
    qkv_grad = qkv_grad.reshape(n_a, n_g, n_r, share, columns)
    qkv_grad = scatter_sum(after(scatter_sum(qkv_grad, "a", 0), first), "r", 1)
    second = jnp.concatenate([second, qkv_grad.astype(BF16)], axis=2)
    second = lax.all_to_all(after(second, first), "g", 0, 0)
    input_grad = input_gradient(scalars, tokens, grad_resid, gain_one[None], qkv_weight, whole)

    first = jnp.sum(first.astype(F32), axis=0)
    out_share = first[:, :width]
    up_share = first[:, width:]
    second_share = jnp.sum(up_turned.astype(F32) * up_share, axis=1)
    up_share = (
        up_share.reshape(share, wide, n_all, share).transpose(0, 2, 1, 3).reshape(share, hidden)
    )
    place = lax.axis_index(ALL) * share
    own_gain_one = lax.dynamic_slice_in_dim(gain_one, place, share)
    own_gain_two = lax.dynamic_slice_in_dim(gain_two, place, share)
    second_share = second_share / own_gain_two
    down_share, qkv_share, first_share = last_shares(
        second, turned.swapaxes(0, 1), own_gain_one[:, None]
    )
    down_share = down_share.reshape(wide * share, width)
    first_share = first_share.reshape(share)
    return (
        mixed,
        input_grad,
        qkv_share,
        out_share,
        up_share,
        down_share,
        first_share,
        second_share,
    )


def solution(mesh):
    n_scene, n_seq = mesh.devices.shape
    n_g = math.gcd(HEADS, n_seq)
    inner = Mesh(mesh.devices.reshape(n_scene // 2, 2, n_g, n_seq // n_g), ALL)
    split = P(ALL, None)
    in_specs = (split, P(("a", "c")), split, split, split, split, split, P(), P())
    out_specs = (split, split, split, split, split, split, P(ALL), P(ALL))
    return jax.shard_map(
        on_device, mesh=inner, in_specs=in_specs, out_specs=out_specs, check_vma=False
    )
```
